256 devices in a mesh: req: 32 (over y, z_hi, core), tp: 8 (over z_lo, x).
Axes of the slice: x: 4, y: 4, z: 8 (z_hi: 4, z_lo: 2; z = z_hi * 2 + z_lo), core: 2. Of those that a mesh axis runs over, the one named last changes fastest.
Arguments:
- tokens: bfloat16 [16384, 2048], P(('req', 'tp')), may hold values from -40 to 40, as said below
- attn_gain: float32 [2048], replicated, may hold values from 0.25 to 1.75
- w_query: bfloat16 [2048, 2048], P(None, 'tp'), may hold values from -0.125 to 0.125
- key_weight: bfloat16 [2048, 1024], P(None, 'tp'), may hold values from -0.125 to 0.125
- value_weight: bfloat16 [2048, 1024], P(None, 'tp'), may hold values from -0.125 to 0.125
- w_headgate: bfloat16 [2048, 16], P(None, 'tp'), may hold values from -0.125 to 0.125
- query_gain: float32 [128], replicated, may hold values from 1.3 to 2
- key_gain: float32 [128], replicated, may hold values from 1.3 to 2
- w_out: bfloat16 [2048, 2048], P('tp'), may hold values from -0.5 to 0.5
- mlp_gain: float32 [2048], replicated, may hold values from 0.25 to 1.75
- w_gate: bfloat16 [2048, 3072], P(None, 'tp'), may hold values from -0.125 to 0.125
- w_up: bfloat16 [2048, 3072], P(None, 'tp'), may hold values from -0.125 to 0.125
- w_down: bfloat16 [3072, 2048], P('tp'), may hold values from -0.109375 to 0.109375
- pooled_keys: bfloat16 [16384, 16, 8, 128], P(('req', 'tp')), may hold values from -150 to 150, as said below
- pooled_values: bfloat16 [16384, 16, 8, 128], P(('req', 'tp')), may hold values from -6 to 6
- sink_key_cache: bfloat16 [64, 4, 8, 128], P('req', None, 'tp'), may hold values from -12 to 12
- sink_value_cache: bfloat16 [64, 4, 8, 128], P('req', None, 'tp'), may hold values from -6 to 6
- cached_length: int32 [64], P('req'), may hold values from 0 to 32768, as said below
- valid_length: int32 [64], P('req'), may hold values from 1 to 256, as said below
- sink_position_count: int32 [64], P('req'), may hold values from 0 to 4, as said below
- window: int32 [64], P('req'), may hold values from 2048 to 4096, as said below
- page_slot: int32 [32, 512], P('req'), may hold values from 0 to 511, each once within a row
Outputs:
- out: float32 [16384, 2048], P(('req', 'tp'))
- app_keys: bfloat16 [16384, 8, 128], P('req', 'tp')
- app_values: bfloat16 [16384, 8, 128], P('req', 'tp')
The draws below stay inside these ranges and needn't reach their ends.
Inputs may be any that keep to these rules, and one draw needn't show every extreme that they name: `tokens`: rows of the input; rows and features have unlike scales. `pooled_keys`: keys as the cache stores them. `cached_length`: short requests lie below 4096; some request has exactly 32768. `valid_length`: the rest of a span is padding; some request has exactly 256. `sink_position_count`: some request has exactly 4. `window`: some request has exactly 4096. `page_slot`: each row is a permutation.
All inputs are finite; a program needn't handle non-finite values.
Results may differ from the reference program's by a relative error of at most 0.02.
The reference program's roundings to bfloat16 on the way count: a program that leaves them out, or rounds other values in their place, can miss the bound.
Values may be sent and summed in bfloat16 or wider, within the bound.
A program may use at most 128 MiB of HBM per device.

```python
import math
import jax
import jax.numpy as jnp
from jax import lax

MODEL_WIDTH = 2048
QUERY_HEADS = 16
KEY_VALUE_HEADS = 8
HEAD_SIZE = 128
FF = 3072
WINDOW_TOKENS = 4096
PAGE_TOKENS = 16
SINK_SLOTS = 4
CTX_MAX = 32768
SPAN_TOKENS = 256
REQ_DEV = 2
REQUEST_COUNT = 64
TOKEN_COUNT = 16384
NPAGE = 256
POOL_PAGE_COUNT = 16384
N_REQ = 32
N_TP = 8


def draw_tokens(key, part):
    leading_key, second_key, third_key = jax.random.split(key, 3)
    sampled_case = jax.random.normal(leading_key, (TOKEN_COUNT, MODEL_WIDTH), jnp.float32) * 0.7
    row_scale = jnp.exp(jax.random.uniform(second_key, (TOKEN_COUNT, 1), jnp.float32, -1.15, 1.15))
    col_scale = jnp.exp(jax.random.uniform(third_key, (1, MODEL_WIDTH), jnp.float32, -1.15, 1.15))
    return jnp.clip(sampled_case * row_scale * col_scale, -40.0, 40.0).astype(jnp.bfloat16)


def draw_pooled_keys(key, part):
    leading_key = jax.random.fold_in(key, 0)
    sampled_case = jnp.clip(jax.random.normal(leading_key, (POOL_PAGE_COUNT, PAGE_TOKENS, KEY_VALUE_HEADS, HEAD_SIZE), jnp.float32) * 1.7, -10.0, 10.0)
    return sampled_case.astype(jnp.bfloat16)


def draw_cached_length(key, part):
    leading_key, second_key, third_key, fourth_key = jax.random.split(key, 4)
    short_len = jax.random.randint(leading_key, (REQUEST_COUNT,), 0, WINDOW_TOKENS)
    long_len = jax.random.randint(second_key, (REQUEST_COUNT,), WINDOW_TOKENS, CTX_MAX + 1)
    selector = jax.random.randint(third_key, (REQUEST_COUNT,), 0, 2)
    lengths = jnp.where(selector == 1, long_len, short_len)
    chosen = jax.random.randint(fourth_key, (), 0, REQUEST_COUNT)
    return jnp.where(jnp.arange(REQUEST_COUNT) == chosen, CTX_MAX, lengths).astype(jnp.int32)


def draw_valid_length(key, part):
    leading_key, second_key = jax.random.split(key)
    counts = jax.random.randint(leading_key, (REQUEST_COUNT,), 1, SPAN_TOKENS + 1)
    chosen = jax.random.randint(second_key, (), 0, REQUEST_COUNT)
    return jnp.where(jnp.arange(REQUEST_COUNT) == chosen, SPAN_TOKENS, counts).astype(jnp.int32)


def draw_sink_position_count(key, part):
    leading_key, second_key = jax.random.split(key)
    counts = jax.random.randint(leading_key, (REQUEST_COUNT,), 0, SINK_SLOTS + 1)
    chosen = jax.random.randint(second_key, (), 0, REQUEST_COUNT)
    return jnp.where(jnp.arange(REQUEST_COUNT) == chosen, SINK_SLOTS, counts).astype(jnp.int32)


def draw_window(key, part):
    leading_key, second_key = jax.random.split(key)
    counts = jax.random.randint(leading_key, (REQUEST_COUNT,), WINDOW_TOKENS // 2, WINDOW_TOKENS + 1)
    chosen = jax.random.randint(second_key, (), 0, REQUEST_COUNT)
    return jnp.where(jnp.arange(REQUEST_COUNT) == chosen, WINDOW_TOKENS, counts).astype(jnp.int32)


def shard_levels(own_key, shape, cuts, least, high):
    loudness, own = 1.0, jax.random.fold_in(own_key, 6)
    for position, blocks in cuts:
        steps = jnp.exp(jax.random.uniform(jax.random.fold_in(own, position), (blocks,), jnp.float32, least / len(cuts), high / len(cuts)))
        loudness = loudness * jnp.repeat(steps, shape[position] // blocks).reshape([-1 if axis == position else 1 for axis in range(len(shape))])
    return loudness


def gaussian(rng, shape, scale, bound, cuts=(), kind=jnp.bfloat16):
    loudness = shard_levels(rng, shape, cuts, -0.22, 0.18) if cuts else 1.0
    entries = jax.random.normal(rng, shape, jnp.float32) * scale * loudness
    return jnp.minimum(jnp.maximum(entries, -bound), bound).astype(kind)


def setup_inputs(seed: int = 0) -> dict:
    splits = jax.random.split(jax.random.key(seed), 23)
    return {
        "tokens": draw_tokens(jax.random.fold_in(splits[22], 71), 0),
        "attn_gain": jnp.clip(1.0 + 0.15 * jax.random.normal(splits[1], (MODEL_WIDTH,), jnp.float32), 0.25, 1.75),
        "w_query": gaussian(splits[2], (MODEL_WIDTH, QUERY_HEADS * HEAD_SIZE), MODEL_WIDTH ** -0.5, 0.125, ((1, 8),)),
        "key_weight": gaussian(splits[3], (MODEL_WIDTH, KEY_VALUE_HEADS * HEAD_SIZE), MODEL_WIDTH ** -0.5, 0.125, ((1, 8),)),
        "value_weight": gaussian(splits[4], (MODEL_WIDTH, KEY_VALUE_HEADS * HEAD_SIZE), MODEL_WIDTH ** -0.5, 0.125, ((1, 8),)),
        "w_headgate": gaussian(splits[5], (MODEL_WIDTH, QUERY_HEADS), MODEL_WIDTH ** -0.5, 0.125, ((1, 8),)),
        "query_gain": jnp.clip(jax.random.uniform(splits[6], (HEAD_SIZE,), jnp.float32, 1.3, 2.0), 1.3, 2.0),
        "key_gain": jnp.clip(jax.random.uniform(splits[7], (HEAD_SIZE,), jnp.float32, 1.3, 2.0), 1.3, 2.0),
        "w_out": gaussian(splits[8], (QUERY_HEADS * HEAD_SIZE, MODEL_WIDTH), (QUERY_HEADS * HEAD_SIZE // 16) ** -0.5, 0.5, ((0, 8),)),
        "mlp_gain": jnp.clip(1.0 + 0.15 * jax.random.normal(splits[9], (MODEL_WIDTH,), jnp.float32), 0.25, 1.75),
        "w_gate": gaussian(splits[10], (MODEL_WIDTH, FF), MODEL_WIDTH ** -0.5, 0.125, ((1, 8),)),
        "w_up": gaussian(splits[11], (MODEL_WIDTH, FF), MODEL_WIDTH ** -0.5, 0.125, ((1, 8),)),
        "w_down": gaussian(splits[12], (FF, MODEL_WIDTH), FF ** -0.5, 0.109375, ((0, 8),)),
        "pooled_keys": draw_pooled_keys(jax.random.fold_in(splits[22], 71), 0),
        "pooled_values": gaussian(splits[14], (POOL_PAGE_COUNT, PAGE_TOKENS, KEY_VALUE_HEADS, HEAD_SIZE), 1.0, 6.0, ((0, 256),)),
        "sink_key_cache": gaussian(splits[15], (REQUEST_COUNT, SINK_SLOTS, KEY_VALUE_HEADS, HEAD_SIZE), 3.0, 12.0, ((0, 32), (2, 8))),
        "sink_value_cache": gaussian(splits[16], (REQUEST_COUNT, SINK_SLOTS, KEY_VALUE_HEADS, HEAD_SIZE), 1.0, 6.0, ((0, 32), (2, 8))),
        "cached_length": draw_cached_length(jax.random.fold_in(splits[22], 71), 0),
        "valid_length": draw_valid_length(jax.random.fold_in(splits[22], 71), 0),
        "sink_position_count": draw_sink_position_count(jax.random.fold_in(splits[22], 71), 0),
        "window": draw_window(jax.random.fold_in(splits[22], 71), 0),
        "page_slot": jax.vmap(lambda own: jax.random.permutation(own, REQ_DEV * NPAGE))(jax.random.split(splits[21], N_REQ)).reshape((N_REQ, REQ_DEV * NPAGE)).astype(jnp.int32),
    }


EPSILON = 1e-06
ROPE_BASE = 1000000.0
NEG_FILL = -1e+30

def rms_rows(values, gain):
    mean_square = lax.optimization_barrier(jnp.mean(values * values, axis=-1, keepdims=True))
    return values * lax.rsqrt(mean_square + EPSILON) * gain

def rotary(heads, positions):
    head_width = heads.shape[-1]
    half_width = head_width // 2
    freqs = ROPE_BASE ** (-2.0 * jnp.arange(half_width, dtype=jnp.float32) / head_width)
    angles = positions.astype(jnp.float32)[:, None] * freqs[None, :]
    cosine = jnp.cos(angles)[:, None, :]
    sine_part = jnp.sin(angles)[:, None, :]
    first_half = heads[..., :half_width]
    second_half = heads[..., half_width:]
    return jnp.concatenate([first_half * cosine - second_half * sine_part, second_half * cosine + first_half * sine_part], axis=-1)

def rounded(values):
    return lax.optimization_barrier(values.astype(jnp.bfloat16)).astype(jnp.float32)

def attend_request(member, pooled_keys, pooled_values):
    query_vectors, fresh_keys, fresh_values, sink_key_rows, sink_value_rows, page_row_list, cached, valid, sinks_used, reach = member
    window_key_rows = pooled_keys[page_row_list].reshape(WINDOW_TOKENS, KEY_VALUE_HEADS, HEAD_SIZE)
    window_value_rows = pooled_values[page_row_list].reshape(WINDOW_TOKENS, KEY_VALUE_HEADS, HEAD_SIZE)
    all_keys = jnp.concatenate([sink_key_rows, window_key_rows, fresh_keys], axis=0).astype(jnp.float32)
    all_values = jnp.concatenate([sink_value_rows, window_value_rows, fresh_values], axis=0).astype(jnp.float32)
    query_row_block = query_vectors.astype(jnp.float32).reshape(SPAN_TOKENS, KEY_VALUE_HEADS, QUERY_HEADS // KEY_VALUE_HEADS, HEAD_SIZE)
    scores = jnp.einsum('ckgd,nkd->ckgn', query_row_block, all_keys, precision=lax.Precision.HIGHEST) * (1.0 / math.sqrt(HEAD_SIZE))
    offsets = jnp.arange(SPAN_TOKENS, dtype=jnp.int32)
    sink_slots = jnp.arange(SINK_SLOTS, dtype=jnp.int32)
    window_slots = jnp.arange(WINDOW_TOKENS, dtype=jnp.int32)
    sink_ok = (sink_slots < sinks_used) & (sink_slots < cached - WINDOW_TOKENS)
    key_positions = cached - WINDOW_TOKENS + window_slots
    window_ok = (key_positions[None, :] >= 0) & ((key_positions[None, :] < sinks_used) | ((WINDOW_TOKENS - window_slots)[None, :] + offsets[:, None] <= reach))
    span_ok = (offsets[None, :] < valid) & (offsets[None, :] <= offsets[:, None]) & ((cached + offsets[None, :] < sinks_used) | (offsets[:, None] - offsets[None, :] <= reach))
    allowed = jnp.concatenate([jnp.broadcast_to(sink_ok[None, :], (SPAN_TOKENS, SINK_SLOTS)), window_ok, span_ok], axis=1)[:, None, None, :]
    highest = lax.optimization_barrier(jnp.max(jnp.where(allowed, scores, NEG_FILL), axis=-1, keepdims=True))
    weights = jnp.where(allowed, jnp.exp(scores - highest), 0.0)
    total = lax.optimization_barrier(jnp.sum(weights, axis=-1))
    summed = jnp.einsum('ckgn,nkd->ckgd', rounded(weights), all_values, precision=lax.Precision.HIGHEST)
    return summed / total[..., None]

def reference(tokens, attn_gain, w_query, key_weight, value_weight, w_headgate, query_gain, key_gain, w_out, mlp_gain, w_gate, w_up, w_down, pooled_keys, pooled_values, sink_key_cache, sink_value_cache, cached_length, valid_length, sink_position_count, window, page_slot):
    residual = tokens.astype(jnp.float32)
    normalized_input = rms_rows(residual, attn_gain).astype(jnp.bfloat16)
    offsets = jnp.arange(SPAN_TOKENS, dtype=jnp.int32)
    positions = (cached_length[:, None] + offsets[None, :]).reshape(TOKEN_COUNT)
    query_vectors = jnp.dot(normalized_input, w_query, preferred_element_type=jnp.float32).reshape(TOKEN_COUNT, QUERY_HEADS, HEAD_SIZE)
    query_vectors = rotary(rms_rows(query_vectors, query_gain), positions).astype(jnp.bfloat16)
    fresh_keys = jnp.dot(normalized_input, key_weight, preferred_element_type=jnp.float32).reshape(TOKEN_COUNT, KEY_VALUE_HEADS, HEAD_SIZE)
    fresh_keys = rotary(rms_rows(fresh_keys, key_gain), positions).astype(jnp.bfloat16)
    fresh_values = jnp.dot(normalized_input, value_weight, preferred_element_type=jnp.float32).astype(jnp.bfloat16).reshape(TOKEN_COUNT, KEY_VALUE_HEADS, HEAD_SIZE)
    headgate = jax.nn.sigmoid(jnp.dot(normalized_input, w_headgate, preferred_element_type=jnp.float32))
    present = (offsets[None, :] < valid_length[:, None]).reshape(TOKEN_COUNT)[:, None, None]
    app_keys = jnp.where(present, fresh_keys, jnp.zeros_like(fresh_keys))
    app_values = jnp.where(present, fresh_values, jnp.zeros_like(fresh_values))
    request_ids = jnp.arange(REQUEST_COUNT, dtype=jnp.int32)
    home_rows = request_ids // REQ_DEV
    within = request_ids % REQ_DEV
    page_ids = jnp.arange(NPAGE, dtype=jnp.int32)
    slot_rows = jnp.take_along_axis(page_slot[home_rows], within[:, None] * NPAGE + page_ids[None, :], axis=1)
    page_row_list = (home_rows[:, None] * (REQ_DEV * NPAGE) + slot_rows).astype(jnp.int32)
    member_rows = (query_vectors.reshape(REQUEST_COUNT, SPAN_TOKENS, QUERY_HEADS, HEAD_SIZE), fresh_keys.reshape(REQUEST_COUNT, SPAN_TOKENS, KEY_VALUE_HEADS, HEAD_SIZE), fresh_values.reshape(REQUEST_COUNT, SPAN_TOKENS, KEY_VALUE_HEADS, HEAD_SIZE), sink_key_cache, sink_value_cache, page_row_list, cached_length, valid_length, sink_position_count, window)
    mixture = lax.map(lambda member: attend_request(member, pooled_keys, pooled_values), member_rows)
    mixture = mixture.reshape(TOKEN_COUNT, QUERY_HEADS, HEAD_SIZE)
    heads_out = (mixture * headgate[..., None]).astype(jnp.bfloat16).reshape(TOKEN_COUNT, QUERY_HEADS * HEAD_SIZE)
    heads_width = QUERY_HEADS * HEAD_SIZE // N_TP
    hidden_width = FF // N_TP
    attn = jnp.zeros((TOKEN_COUNT, MODEL_WIDTH), jnp.float32)
    for shard_index in range(N_TP):
        row_start = shard_index * heads_width
        attn = attn + rounded(jnp.dot(heads_out[:, row_start:row_start + heads_width], w_out[row_start:row_start + heads_width], preferred_element_type=jnp.float32))
    middle = residual + attn
    normed_mid = rms_rows(middle, mlp_gain).astype(jnp.bfloat16)
    branch = jnp.zeros((TOKEN_COUNT, MODEL_WIDTH), jnp.float32)
    for shard_index in range(N_TP):
        row_start = shard_index * hidden_width
        gate_part = jnp.dot(normed_mid, w_gate[:, row_start:row_start + hidden_width], preferred_element_type=jnp.float32)
        up_part = jnp.dot(normed_mid, w_up[:, row_start:row_start + hidden_width], preferred_element_type=jnp.float32)
        hidden = (jax.nn.silu(gate_part) * up_part).astype(jnp.bfloat16)
        branch = branch + rounded(jnp.dot(hidden, w_down[row_start:row_start + hidden_width], preferred_element_type=jnp.float32))
    return (middle + branch, app_keys, app_values)
```

```python
import math

import jax
import jax.numpy as jnp
from jax import lax
from jax.experimental import pallas as pl
from jax.experimental.pallas import tpu as pltpu
from jax.sharding import PartitionSpec as P

WINDOW_TOKENS = 4096
SPAN_TOKENS = 256


EPSILON = 1e-06
ROPE_BASE = 1000000.0
NEG_FILL = -1e30


def rms_rows(values, gain):
    mean_square = jnp.mean(values * values, axis=-1, keepdims=True)
    return values * lax.rsqrt(mean_square + EPSILON) * gain


def rotary(heads, positions):
    head_width = heads.shape[-1]
    half_width = head_width // 2
    freqs = ROPE_BASE ** (-2.0 * jnp.arange(half_width, dtype=jnp.float32) / head_width)
    angles = positions.astype(jnp.float32)[:, None] * freqs[None, :]
    cosine = jnp.cos(angles)[:, None, :]
    sine_part = jnp.sin(angles)[:, None, :]
    first_half = heads[..., :half_width]
    second_half = heads[..., half_width:]
    return jnp.concatenate(
        [
            first_half * cosine - second_half * sine_part,
            second_half * cosine + first_half * sine_part,
        ],
        axis=-1,
    )


def masked_max(scores, allowed):
    return jnp.max(jnp.where(allowed, scores, NEG_FILL), axis=-1)


def near_masks(cached, valid, sinks_used, reach, span_len, window_len, sink_len):
    offsets = jnp.arange(span_len, dtype=jnp.int32)
    sink_slots = jnp.arange(sink_len, dtype=jnp.int32)
    sink_ok = (sink_slots[None, :] < sinks_used[:, None]) & (
        sink_slots[None, :] < (cached - window_len)[:, None]
    )
    span_ok = (
        (offsets[None, None, :] < valid[:, None, None])
        & (offsets[None, None, :] <= offsets[None, :, None])
        & (
            (cached[:, None, None] + offsets[None, None, :] < sinks_used[:, None, None])
            | (offsets[None, :, None] - offsets[None, None, :] <= reach[:, None, None])
        )
    )
    return (sink_ok[:, None, None, None, :], span_ok[:, :, None, None, :])


def near_scores(query_vectors, sink_key_rows, fresh_keys, score_scale):
    sink_scores = (
        jnp.einsum(
            "rckgd,rskd->rckgs", query_vectors, sink_key_rows, preferred_element_type=jnp.float32
        )
        * score_scale
    )
    span_scores = (
        jnp.einsum(
            "rckgd,rtkd->rckgt", query_vectors, fresh_keys, preferred_element_type=jnp.float32
        )
        * score_scale
    )
    return (sink_scores, span_scores)


def attend_whole(
    query_vectors,
    sink_key_rows,
    sink_value_rows,
    window_key_rows,
    window_value_rows,
    fresh_keys,
    fresh_values,
    cached,
    valid,
    sinks_used,
    reach,
    score_scale,
):
    span_len = query_vectors.shape[1]
    window_len = window_key_rows.shape[1]
    sink_ok, span_ok = near_masks(
        cached, valid, sinks_used, reach, span_len, window_len, sink_key_rows.shape[1]
    )
    offsets = jnp.arange(span_len, dtype=jnp.int32)
    window_slots = jnp.arange(window_len, dtype=jnp.int32)
    key_positions = cached[:, None] - window_len + window_slots[None, :]
    window_ok = (key_positions[:, None, :] >= 0) & (
        (key_positions[:, None, :] < sinks_used[:, None, None])
        | (
            (window_len - window_slots)[None, None, :] + offsets[None, :, None]
            <= reach[:, None, None]
        )
    )
    window_ok = window_ok[:, :, None, None, :]
    sink_scores, span_scores = near_scores(query_vectors, sink_key_rows, fresh_keys, score_scale)
    window_scores = (
        jnp.einsum(
            "rckgd,rwkd->rckgw", query_vectors, window_key_rows, preferred_element_type=jnp.float32
        )
        * score_scale
    )
    highest = jnp.maximum(
        jnp.maximum(masked_max(sink_scores, sink_ok), masked_max(window_scores, window_ok)),
        masked_max(span_scores, span_ok),
    )[..., None]
    sink_weights = jnp.where(sink_ok, jnp.exp(sink_scores - highest), 0.0)
    window_weights = jnp.where(window_ok, jnp.exp(window_scores - highest), 0.0)
    span_weights = jnp.where(span_ok, jnp.exp(span_scores - highest), 0.0)
    total = (
        jnp.sum(sink_weights, axis=-1)
        + jnp.sum(window_weights, axis=-1)
        + jnp.sum(span_weights, axis=-1)
    )
    summed = jnp.einsum(
        "rckgs,rskd->rckgd",
        sink_weights.astype(jnp.bfloat16),
        sink_value_rows,
        preferred_element_type=jnp.float32,
    )
    summed = summed + jnp.einsum(
        "rckgw,rwkd->rckgd",
        window_weights.astype(jnp.bfloat16),
        window_value_rows,
        preferred_element_type=jnp.float32,
    )
    summed = summed + jnp.einsum(
        "rckgt,rtkd->rckgd",
        span_weights.astype(jnp.bfloat16),
        fresh_values,
        preferred_element_type=jnp.float32,
    )
    return summed / total[..., None]


MESH = pl.DeviceIdType.MESH
ROWS = 64
WIDTH = 2048


def ring_place(shift, flip):
    t = lax.axis_index("tp")
    x = lax.rem(t, 4)
    z = t // 4
    plane = 1 - z if flip else z
    return lax.rem(x + shift, 4) + 4 * plane


def row_window(owner, first, count):
    return pl.ds(pl.multiple_of(owner * ROWS + first, 16), count)


class Mailer:
    def __init__(self, send_sems, recv_sems):
        self.send_sems, self.recv_sems = send_sems, recv_sems
        self.slots = {}
        self.sent = []

    def slot(self, name):
        return self.slots.setdefault(name, len(self.slots))

    def send(self, name, src, dst, target):
        k = self.slot(name)
        copy = pltpu.make_async_remote_copy(
            src_ref=src,
            dst_ref=dst,
            send_sem=self.send_sems.at[k],
            recv_sem=self.recv_sems.at[k],
            device_id={"tp": target},
            device_id_type=MESH,
        )
        copy.start()
        self.sent.append(copy)

    def wait(self, name, dst):
        k = self.slot(name)
        pltpu.make_async_remote_copy(
            src_ref=dst,
            dst_ref=dst,
            send_sem=self.send_sems.at[k],
            recv_sem=self.recv_sems.at[k],
            device_id={"tp": ring_place(0, True)},
            device_id_type=MESH,
        ).wait_recv()

    def drain(self):
        for copy in self.sent:
            copy.wait_send()
        self.sent = []


def meet_neighbours():
    barrier = pltpu.get_barrier_semaphore()
    for shift, flip in ((1, False), (3, False), (0, True)):
        pl.semaphore_signal(
            barrier, inc=1, device_id={"tp": ring_place(shift, flip)}, device_id_type=MESH
        )
    pl.semaphore_wait(barrier, 3)


def add_into(part, owner, first, count, arrived):
    rows = row_window(owner, first, count)
    part[rows, :] = (
        part[rows, :].astype(jnp.float32) + arrived[...].astype(jnp.float32)
    ).astype(jnp.bfloat16)


class Scatter:
    def __init__(self, mail, tag, part, h1, h2, zb, b1, b2, za):
        self.mail, self.tag, self.part = mail, tag, part
        self.h1, self.h2, self.zb, self.b1, self.b2, self.za = h1, h2, zb, b1, b2, za
        self.right, self.left, self.across = ring_place(1, False), ring_place(3, False), ring_place(0, True)

    def rows(self, shift, flip, first, count):
        return self.part.at[row_window(ring_place(shift, flip), first, count), :]

    def put(self, name, src, dst, target):
        self.mail.send(self.tag + name, src, dst, target)

    def got(self, name, dst):
        self.mail.wait(self.tag + name, dst)

    def start_x(self, flip):
        f = int(flip)
        self.put(f"h1r{f}", self.rows(2, flip, 0, 16), self.h1.at[0, f], self.right)
        self.put(f"h1l{f}", self.rows(2, flip, 16, 16), self.h1.at[1, f], self.left)
        self.put(f"h2r{f}1", self.rows(1, flip, 16, 16), self.h2.at[0, f, 1], self.right)
        self.put(f"h2l{f}0", self.rows(3, flip, 0, 16), self.h2.at[1, f, 0], self.left)

    def start_z(self):
        for k, shift in enumerate((2, 1, 3, 0)):
            self.put(f"zb{k}", self.rows(shift, True, 32, 32), self.zb.at[k], self.across)

    def relay_x(self, flip):
        f = int(flip)
        self.got(f"h1r{f}", self.h1.at[0, f])
        add_into(self.part, ring_place(1, flip), 0, 16, self.h1.at[0, f])
        self.put(f"h2r{f}0", self.rows(1, flip, 0, 16), self.h2.at[0, f, 0], self.right)
        self.got(f"h1l{f}", self.h1.at[1, f])
        add_into(self.part, ring_place(3, flip), 16, 16, self.h1.at[1, f])
        self.put(f"h2l{f}1", self.rows(3, flip, 16, 16), self.h2.at[1, f, 1], self.left)

    def relay_z(self):
        self.got("zb0", self.zb.at[0])
        add_into(self.part, ring_place(2, False), 32, 32, self.zb.at[0])
        self.put("b1r", self.rows(2, False, 32, 16), self.b1.at[0], self.right)
        self.put("b1l", self.rows(2, False, 48, 16), self.b1.at[1], self.left)
        self.got("zb1", self.zb.at[1])
        add_into(self.part, ring_place(1, False), 32, 32, self.zb.at[1])
        self.put("b2r1", self.rows(1, False, 48, 16), self.b2.at[0, 1], self.right)
        self.got("zb2", self.zb.at[2])
        add_into(self.part, ring_place(3, False), 32, 32, self.zb.at[2])
        self.put("b2l0", self.rows(3, False, 32, 16), self.b2.at[1, 0], self.left)

    def finish_relays(self):
        for side, letter in ((0, "r"), (1, "l")):
            for half in (0, 1):
                self.got(f"h2{letter}1{half}", self.h2.at[side, 1, half])
        rows = row_window(self.across, 0, 32)
        self.part[rows, :] = (
            self.part[rows, :].astype(jnp.float32)
            + self.h2[0, 1].reshape(32, WIDTH).astype(jnp.float32)
            + self.h2[1, 1].reshape(32, WIDTH).astype(jnp.float32)
        ).astype(jnp.bfloat16)
        self.put("za", self.rows(0, True, 0, 32), self.za, self.across)
        self.got("b1r", self.b1.at[0])
        add_into(self.part, ring_place(1, False), 32, 16, self.b1.at[0])
        self.put("b2r0", self.rows(1, False, 32, 16), self.b2.at[0, 0], self.right)
        self.got("b1l", self.b1.at[1])
        add_into(self.part, ring_place(3, False), 48, 16, self.b1.at[1])
        self.put("b2l1", self.rows(3, False, 48, 16), self.b2.at[1, 1], self.left)

    def total(self):
        me = ring_place(0, False)
        f32 = jnp.float32
        for side, letter in ((0, "r"), (1, "l")):
            for half in (0, 1):
                self.got(f"h2{letter}0{half}", self.h2.at[side, 0, half])
        upper = (
            self.part[row_window(me, 0, 32), :].astype(f32)
            + self.h2[0, 0].reshape(32, WIDTH).astype(f32)
            + self.h2[1, 0].reshape(32, WIDTH).astype(f32)
        )
        self.got("zb3", self.zb.at[3])
        lower = self.part[row_window(me, 32, 32), :].astype(f32) + self.zb[3].astype(f32)
        for side, letter in ((0, "r"), (1, "l")):
            for half in (0, 1):
                self.got(f"b2{letter}{half}", self.b2.at[side, half])
        lower = (
            lower
            + self.b2[0].reshape(32, WIDTH).astype(f32)
            + self.b2[1].reshape(32, WIDTH).astype(f32)
        )
        self.got("za", self.za)
        upper = upper + self.za[...].astype(f32)
        return upper, lower


SCATTER_BUFFERS = [
    ((2, 2, 16, WIDTH)),
    ((2, 2, 2, 16, WIDTH)),
    ((4, 32, WIDTH)),
    ((2, 16, WIDTH)),
    ((2, 2, 16, WIDTH)),
    ((32, WIDTH)),
]
SCATTER_COPIES = 24


class Gather:
    def __init__(self, mail, tag, rows):
        self.mail, self.tag, self.rows = mail, tag, rows
        self.right, self.left, self.across = ring_place(1, False), ring_place(3, False), ring_place(0, True)

    def part(self, shift, flip, first, count):
        return self.rows.at[row_window(ring_place(shift, flip), first, count), :]

    def put(self, name, place, target):
        ref = self.part(*place)
        self.mail.send(self.tag + name, ref, ref, target)

    def got(self, name, place):
        self.mail.wait(self.tag + name, self.part(*place))

    def start(self):
        self.put("z0", (0, False, 0, 32), self.across)
        self.put("r0", (0, False, 32, 32), self.right)
        self.put("l0", (0, False, 32, 32), self.left)
        self.put("r1", (0, False, 0, 32), self.right)
        self.put("l1", (0, False, 0, 32), self.left)
        self.put("z1", (0, False, 32, 32), self.across)

    def relay_near(self):
        self.got("r0", (3, False, 32, 32))
        self.put("r2", (3, False, 32, 16), self.right)
        self.put("z2", (3, False, 32, 32), self.across)
        self.got("l0", (1, False, 32, 32))
        self.put("l2", (1, False, 48, 16), self.left)
        self.put("z3", (1, False, 32, 32), self.across)
        self.got("r1", (3, False, 0, 32))
        self.put("r4", (3, False, 0, 16), self.right)
        self.got("l1", (1, False, 0, 32))
        self.put("l4", (1, False, 16, 16), self.left)
        self.got("z0", (0, True, 0, 32))
        self.put("r3", (0, True, 0, 32), self.right)
        self.put("l3", (0, True, 0, 32), self.left)
        self.got("r2", (2, False, 32, 16))
        self.put("z4", (2, False, 32, 16), self.across)
        self.got("l2", (2, False, 48, 16))
        self.put("z5", (2, False, 48, 16), self.across)
        self.got("r4", (2, False, 0, 16))
        self.got("l4", (2, False, 16, 16))

    def relay_far(self):
        self.got("r3", (3, True, 0, 32))
        self.put("r5", (3, True, 0, 16), self.right)
        self.got("l3", (1, True, 0, 32))
        self.put("l5", (1, True, 16, 16), self.left)

    def finish(self):
        self.got("r5", (2, True, 0, 16))
        self.got("l5", (2, True, 16, 16))
        self.got("z1", (0, True, 32, 32))
        self.got("z2", (3, True, 32, 32))
        self.got("z3", (1, True, 32, 32))
        self.got("z4", (2, True, 32, 16))
        self.got("z5", (2, True, 48, 16))


GATHER_COPIES = 18


def tail_kernel(
    heads_ref,
    tokens_ref,
    gain_ref,
    w_out_ref,
    w_gate_ref,
    w_up_ref,
    w_down_ref,
    out_ref,
    w_out_vmem,
    w_both_vmem,
    w_down_vmem,
    part_one,
    part_two,
    rows_mid,
    middle,
    *rest,
):
    buffers_one, buffers_two = rest[:6], rest[6:12]
    load_sems, send_sems, recv_sems = rest[12:]
    units = w_down_ref.shape[0]
    loads = [
        pltpu.make_async_copy(w_out_ref, w_out_vmem, load_sems.at[0]),
        pltpu.make_async_copy(w_gate_ref, w_both_vmem.at[:, :units], load_sems.at[1]),
        pltpu.make_async_copy(w_up_ref, w_both_vmem.at[:, units:], load_sems.at[2]),
        pltpu.make_async_copy(w_down_ref, w_down_vmem, load_sems.at[3]),
    ]
    for load in loads:
        load.start()
    meet_neighbours()
    mail = Mailer(send_sems, recv_sems)
    plane = lax.axis_index("tp") // 4
    half_rows = 4 * ROWS

    def half(flip):
        return pl.ds(pl.multiple_of((1 - plane if flip else plane) * half_rows, half_rows), half_rows)

    scatter = Scatter(mail, "a", part_one, *buffers_one)
    loads[0].wait()

    def project(flip):
        rows = half(flip)
        part_one[rows, :] = jnp.dot(
            heads_ref[rows, :], w_out_vmem[...], preferred_element_type=jnp.float32
        ).astype(jnp.bfloat16)

    project(True)
    scatter.start_z()
    scatter.start_x(True)
    project(False)
    scatter.start_x(False)
    scatter.relay_x(True)
    scatter.relay_x(False)
    scatter.relay_z()
    scatter.finish_relays()
    upper, lower = scatter.total()
    me = ring_place(0, False)
    for first, attn in ((0, upper), (32, lower)):
        mid = tokens_ref[first : first + 32, :].astype(jnp.float32) + attn
        middle[first : first + 32, :] = mid
        mean_square = jnp.mean(mid * mid, axis=-1, keepdims=True)
        rows_mid[row_window(me, first, 32), :] = (
            mid * lax.rsqrt(mean_square + EPSILON) * gain_ref[...]
        ).astype(jnp.bfloat16)
    gather = Gather(mail, "g", rows_mid)
    gather.start()
    gather.relay_near()
    for load in loads[1:]:
        load.wait()

    def feed(flip):
        rows = half(flip)
        both = jnp.dot(rows_mid[rows, :], w_both_vmem[...], preferred_element_type=jnp.float32)
        gate, up = both[:, :units], both[:, units:]
        hidden = (gate / (1.0 + jnp.exp(-gate)) * up).astype(jnp.bfloat16)
        part_two[rows, :] = jnp.dot(
            hidden, w_down_vmem[...], preferred_element_type=jnp.float32
        ).astype(jnp.bfloat16)

    scatter = Scatter(mail, "b", part_two, *buffers_two)
    gather.relay_far()
    feed(False)
    scatter.start_x(False)
    gather.finish()
    feed(True)
    scatter.start_z()
    scatter.start_x(True)
    scatter.relay_x(False)
    scatter.relay_x(True)
    scatter.relay_z()
    scatter.finish_relays()
    upper, lower = scatter.total()
    out_ref[0:32, :] = middle[0:32, :] + upper
    out_ref[32:64, :] = middle[32:64, :] + lower
    mail.drain()


def layer_tail(heads_out, tokens, mlp_gain, w_out, w_gate, w_up, w_down):
    rows_total = heads_out.shape[0]
    bf16 = jnp.bfloat16
    vmem = pl.BlockSpec(memory_space=pltpu.VMEM)
    hbm = pl.BlockSpec(memory_space=pl.ANY)
    buffers = [pltpu.VMEM(shape, bf16) for shape in SCATTER_BUFFERS]
    copies = 2 * SCATTER_COPIES + GATHER_COPIES
    return pl.pallas_call(
        tail_kernel,
        out_shape=jax.ShapeDtypeStruct(tokens.shape, jnp.float32),
        in_specs=[vmem, vmem, vmem, hbm, hbm, hbm, hbm],
        out_specs=vmem,
        scratch_shapes=[
            pltpu.VMEM(w_out.shape, bf16),
            pltpu.VMEM((w_gate.shape[0], 2 * w_gate.shape[1]), bf16),
            pltpu.VMEM(w_down.shape, bf16),
            pltpu.VMEM((rows_total, WIDTH), bf16),
            pltpu.VMEM((rows_total, WIDTH), bf16),
            pltpu.VMEM((rows_total, WIDTH), bf16),
            pltpu.VMEM(tokens.shape, jnp.float32),
            *buffers,
            *buffers,
            pltpu.SemaphoreType.DMA((4,)),
            pltpu.SemaphoreType.DMA((copies,)),
            pltpu.SemaphoreType.DMA((copies,)),
        ],
        compiler_params=pltpu.CompilerParams(
            collective_id=1, has_side_effects=True, vmem_limit_bytes=56 * 1024 * 1024
        ),
        name="layer_tail",
    )(heads_out, tokens, mlp_gain[None, :], w_out, w_gate, w_up, w_down)


def body(
    tokens,
    attn_gain,
    w_query,
    key_weight,
    value_weight,
    w_headgate,
    query_gain,
    key_gain,
    w_out,
    mlp_gain,
    w_gate,
    w_up,
    w_down,
    pooled_keys,
    pooled_values,
    sink_key_cache,
    sink_value_cache,
    cached_length,
    valid_length,
    sink_position_count,
    window,
    page_slot,
):
    head_dim = query_gain.shape[0]
    heads_dev = w_query.shape[1] // head_dim
    kv_dev = key_weight.shape[1] // head_dim
    group_size = heads_dev // kv_dev
    requests_dev = cached_length.shape[0]
    window_len = WINDOW_TOKENS
    span_len = SPAN_TOKENS
    score_scale = 1.0 / math.sqrt(head_dim)
    all_rows = lax.all_gather(tokens, "tp", axis=0, tiled=True)
    residual = all_rows.astype(jnp.float32)
    normalized_input = rms_rows(residual, attn_gain).astype(jnp.bfloat16)
    rows_total = normalized_input.shape[0]
    offsets = jnp.arange(span_len, dtype=jnp.int32)
    positions = (cached_length[:, None] + offsets[None, :]).reshape(rows_total)
    query_vectors = jnp.dot(normalized_input, w_query, preferred_element_type=jnp.float32).reshape(
        rows_total, heads_dev, head_dim
    )
    query_vectors = rotary(rms_rows(query_vectors, query_gain), positions).astype(jnp.bfloat16)
    fresh_keys = jnp.dot(normalized_input, key_weight, preferred_element_type=jnp.float32).reshape(
        rows_total, kv_dev, head_dim
    )
    fresh_keys = rotary(rms_rows(fresh_keys, key_gain), positions).astype(jnp.bfloat16)
    fresh_values = (
        jnp.dot(normalized_input, value_weight, preferred_element_type=jnp.float32)
        .astype(jnp.bfloat16)
        .reshape(rows_total, kv_dev, head_dim)
    )
    headgate = jax.nn.sigmoid(
        jnp.dot(normalized_input, w_headgate, preferred_element_type=jnp.float32)
    )
    present = (offsets[None, :] < valid_length[:, None]).reshape(rows_total)[:, None, None]
    app_keys = jnp.where(present, fresh_keys, jnp.zeros_like(fresh_keys))
    app_values = jnp.where(present, fresh_values, jnp.zeros_like(fresh_values))
    query_blocks = query_vectors.reshape(requests_dev, span_len, kv_dev, group_size, head_dim)
    key_blocks = fresh_keys.reshape(requests_dev, span_len, kv_dev, head_dim)
    value_blocks = fresh_values.reshape(requests_dev, span_len, kv_dev, head_dim)
    arrived_keys, arrived_values = (
        lax.all_to_all(pooled_keys, "tp", split_axis=2, concat_axis=0, tiled=True),
        lax.all_to_all(pooled_values, "tp", split_axis=2, concat_axis=0, tiled=True),
    )
    window_key_rows = jnp.take(arrived_keys, page_slot[0], axis=0).reshape(
        requests_dev, window_len, kv_dev, head_dim
    )
    window_value_rows = jnp.take(arrived_values, page_slot[0], axis=0).reshape(
        requests_dev, window_len, kv_dev, head_dim
    )
    mixture = attend_whole(
        query_blocks,
        sink_key_cache,
        sink_value_cache,
        window_key_rows,
        window_value_rows,
        key_blocks,
        value_blocks,
        cached_length,
        valid_length,
        sink_position_count,
        window,
        score_scale,
    )
    mixture = mixture.reshape(rows_total, heads_dev, head_dim)
    heads_out = (
        (mixture * headgate[..., None])
        .astype(jnp.bfloat16)
        .reshape(rows_total, heads_dev * head_dim)
    )
    output = layer_tail(heads_out, tokens, mlp_gain, w_out, w_gate, w_up, w_down)
    return (output, app_keys, app_values)


def solution(mesh):
    in_specs = (
        P(("req", "tp"), None),
        P(),
        P(None, "tp"),
        P(None, "tp"),
        P(None, "tp"),
        P(None, "tp"),
        P(),
        P(),
        P("tp", None),
        P(),
        P(None, "tp"),
        P(None, "tp"),
        P("tp", None),
        P(("req", "tp"), None, None, None),
        P(("req", "tp"), None, None, None),
        P("req", None, "tp", None),
        P("req", None, "tp", None),
        P("req"),
        P("req"),
        P("req"),
        P("req"),
        P("req", None),
    )
    out_specs = (P(("req", "tp"), None), P("req", "tp", None), P("req", "tp", None))
    return jax.shard_map(body, mesh=mesh, in_specs=in_specs, out_specs=out_specs, check_vma=False)
```

```python
import functools
import math

import jax
import jax.numpy as jnp
import numpy as np
from jax import lax
from jax.experimental import pallas as pl
from jax.experimental.pallas import tpu as pltpu
from jax.sharding import PartitionSpec as P

WINDOW_TOKENS = 4096
SPAN_TOKENS = 256


EPSILON = 1e-06
ROPE_BASE = 1000000.0
NEG_FILL = -1e30

MESH = pl.DeviceIdType.MESH
ROWS = 64
WIDTH = 2048
PEERS = ((1, False), (3, False), (0, True), (1, True), (3, True))


def ring_place(shift, flip):
    t = lax.axis_index("tp")
    x = lax.rem(t, 4)
    z = t // 4
    plane = 1 - z if flip else z
    return lax.rem(x + shift, 4) + 4 * plane


def row_window(owner, first, count):
    return pl.ds(pl.multiple_of(owner * ROWS + first, 16), count)


class Mailer:
    def __init__(self, send_sems, recv_sems):
        self.send_sems, self.recv_sems = send_sems, recv_sems
        self.slots = {}
        self.sent = []

    def slot(self, name):
        return self.slots.setdefault(name, len(self.slots))

    def send(self, name, src, dst, target):
        k = self.slot(name)
        copy = pltpu.make_async_remote_copy(
            src_ref=src,
            dst_ref=dst,
            send_sem=self.send_sems.at[k],
            recv_sem=self.recv_sems.at[k],
            device_id={"tp": target},
            device_id_type=MESH,
        )
        copy.start()
        self.sent.append(copy)

    def wait(self, name, dst):
        k = self.slot(name)
        pltpu.make_async_remote_copy(
            src_ref=dst,
            dst_ref=dst,
            send_sem=self.send_sems.at[k],
            recv_sem=self.recv_sems.at[k],
            device_id={"tp": ring_place(0, True)},
            device_id_type=MESH,
        ).wait_recv()

    def drain(self):
        for copy in self.sent:
            copy.wait_send()
        self.sent = []


def meet_neighbours():
    barrier = pltpu.get_barrier_semaphore()
    for shift, flip in PEERS:
        pl.semaphore_signal(
            barrier, inc=1, device_id={"tp": ring_place(shift, flip)}, device_id_type=MESH
        )
    pl.semaphore_wait(barrier, len(PEERS))


def add_into(part, owner, first, count, arrived):
    rows = row_window(owner, first, count)
    part[rows, :] = (
        part[rows, :].astype(jnp.float32) + arrived[...].astype(jnp.float32)
    ).astype(jnp.bfloat16)


class Scatter:
    def __init__(self, mail, tag, part, h1, h2, zb, b1, b2, za):
        self.mail, self.tag, self.part = mail, tag, part
        self.h1, self.h2, self.zb, self.b1, self.b2, self.za = h1, h2, zb, b1, b2, za
        self.right, self.left, self.across = ring_place(1, False), ring_place(3, False), ring_place(0, True)

    def rows(self, shift, flip, first, count):
        return self.part.at[row_window(ring_place(shift, flip), first, count), :]

    def put(self, name, src, dst, target):
        self.mail.send(self.tag + name, src, dst, target)

    def got(self, name, dst):
        self.mail.wait(self.tag + name, dst)

    def start_x(self, flip):
        f = int(flip)
        self.put(f"h1r{f}", self.rows(2, flip, 0, 16), self.h1.at[0, f], self.right)
        self.put(f"h1l{f}", self.rows(2, flip, 16, 16), self.h1.at[1, f], self.left)
        self.put(f"h2r{f}1", self.rows(1, flip, 16, 16), self.h2.at[0, f, 1], self.right)
        self.put(f"h2l{f}0", self.rows(3, flip, 0, 16), self.h2.at[1, f, 0], self.left)

    def start_z(self):
        for k, shift in enumerate((2, 1, 3, 0)):
            self.put(f"zb{k}", self.rows(shift, True, 32, 32), self.zb.at[k], self.across)

    def relay_x(self, flip):
        f = int(flip)
        self.got(f"h1r{f}", self.h1.at[0, f])
        add_into(self.part, ring_place(1, flip), 0, 16, self.h1.at[0, f])
        self.put(f"h2r{f}0", self.rows(1, flip, 0, 16), self.h2.at[0, f, 0], self.right)
        self.got(f"h1l{f}", self.h1.at[1, f])
        add_into(self.part, ring_place(3, flip), 16, 16, self.h1.at[1, f])
        self.put(f"h2l{f}1", self.rows(3, flip, 16, 16), self.h2.at[1, f, 1], self.left)

    def relay_z(self):
        self.got("zb0", self.zb.at[0])
        add_into(self.part, ring_place(2, False), 32, 32, self.zb.at[0])
        self.put("b1r", self.rows(2, False, 32, 16), self.b1.at[0], self.right)
        self.put("b1l", self.rows(2, False, 48, 16), self.b1.at[1], self.left)
        self.got("zb1", self.zb.at[1])
        add_into(self.part, ring_place(1, False), 32, 32, self.zb.at[1])
        self.put("b2r1", self.rows(1, False, 48, 16), self.b2.at[0, 1], self.right)
        self.got("zb2", self.zb.at[2])
        add_into(self.part, ring_place(3, False), 32, 32, self.zb.at[2])
        self.put("b2l0", self.rows(3, False, 32, 16), self.b2.at[1, 0], self.left)

    def finish_relays(self):
        for side, letter in ((0, "r"), (1, "l")):
            for half in (0, 1):
                self.got(f"h2{letter}1{half}", self.h2.at[side, 1, half])
        rows = row_window(self.across, 0, 32)
        self.part[rows, :] = (
            self.part[rows, :].astype(jnp.float32)
            + self.h2[0, 1].reshape(32, WIDTH).astype(jnp.float32)
            + self.h2[1, 1].reshape(32, WIDTH).astype(jnp.float32)
        ).astype(jnp.bfloat16)
        self.put("za", self.rows(0, True, 0, 32), self.za, self.across)
        self.got("b1r", self.b1.at[0])
        add_into(self.part, ring_place(1, False), 32, 16, self.b1.at[0])
        self.put("b2r0", self.rows(1, False, 32, 16), self.b2.at[0, 0], self.right)
        self.got("b1l", self.b1.at[1])
        add_into(self.part, ring_place(3, False), 48, 16, self.b1.at[1])
        self.put("b2l1", self.rows(3, False, 48, 16), self.b2.at[1, 1], self.left)

    def total(self):
        me = ring_place(0, False)
        f32 = jnp.float32
        for side, letter in ((0, "r"), (1, "l")):
            for half in (0, 1):
                self.got(f"h2{letter}0{half}", self.h2.at[side, 0, half])
        upper = (
            self.part[row_window(me, 0, 32), :].astype(f32)
            + self.h2[0, 0].reshape(32, WIDTH).astype(f32)
            + self.h2[1, 0].reshape(32, WIDTH).astype(f32)
        )
        self.got("zb3", self.zb.at[3])
        lower = self.part[row_window(me, 32, 32), :].astype(f32) + self.zb[3].astype(f32)
        for side, letter in ((0, "r"), (1, "l")):
            for half in (0, 1):
                self.got(f"b2{letter}{half}", self.b2.at[side, half])
        lower = (
            lower
            + self.b2[0].reshape(32, WIDTH).astype(f32)
            + self.b2[1].reshape(32, WIDTH).astype(f32)
        )
        self.got("za", self.za)
        upper = upper + self.za[...].astype(f32)
        return upper, lower


SCATTER_BUFFERS = [
    ((2, 2, 16, WIDTH)),
    ((2, 2, 2, 16, WIDTH)),
    ((4, 32, WIDTH)),
    ((2, 16, WIDTH)),
    ((2, 2, 16, WIDTH)),
    ((32, WIDTH)),
]
SCATTER_COPIES = 24


class Gather:
    def __init__(self, mail, tag, rows):
        self.mail, self.tag, self.rows = mail, tag, rows
        self.right, self.left, self.across = ring_place(1, False), ring_place(3, False), ring_place(0, True)

    def part(self, shift, flip, first, count):
        return self.rows.at[row_window(ring_place(shift, flip), first, count), :]

    def put(self, name, place, target):
        ref = self.part(*place)
        self.mail.send(self.tag + name, ref, ref, target)

    def got(self, name, place):
        self.mail.wait(self.tag + name, self.part(*place))

    def start(self):
        self.put("z0", (0, False, 0, 32), self.across)
        self.put("r0", (0, False, 32, 32), self.right)
        self.put("l0", (0, False, 32, 32), self.left)
        self.put("r1", (0, False, 0, 32), self.right)
        self.put("l1", (0, False, 0, 32), self.left)
        self.put("z1", (0, False, 32, 32), self.across)

    def relay_near(self):
        self.got("r0", (3, False, 32, 32))
        self.put("r2", (3, False, 32, 16), self.right)
        self.put("z2", (3, False, 32, 32), self.across)
        self.got("l0", (1, False, 32, 32))
        self.put("l2", (1, False, 48, 16), self.left)
        self.put("z3", (1, False, 32, 32), self.across)
        self.got("r1", (3, False, 0, 32))
        self.put("r4", (3, False, 0, 16), self.right)
        self.got("l1", (1, False, 0, 32))
        self.put("l4", (1, False, 16, 16), self.left)
        self.got("z0", (0, True, 0, 32))
        self.put("r3", (0, True, 0, 32), self.right)
        self.put("l3", (0, True, 0, 32), self.left)
        self.got("r2", (2, False, 32, 16))
        self.put("z4", (2, False, 32, 16), self.across)
        self.got("l2", (2, False, 48, 16))
        self.put("z5", (2, False, 48, 16), self.across)
        self.got("r4", (2, False, 0, 16))
        self.got("l4", (2, False, 16, 16))

    def relay_far(self):
        self.got("r3", (3, True, 0, 32))
        self.put("r5", (3, True, 0, 16), self.right)
        self.got("l3", (1, True, 0, 32))
        self.put("l5", (1, True, 16, 16), self.left)

    def finish(self):
        self.got("r5", (2, True, 0, 16))
        self.got("l5", (2, True, 16, 16))
        self.got("z1", (0, True, 32, 32))
        self.got("z2", (3, True, 32, 32))
        self.got("z3", (1, True, 32, 32))
        self.got("z4", (2, True, 32, 16))
        self.got("z5", (2, True, 48, 16))


GATHER_COPIES = 18


PAGE = 16
NEAR = 384
BLOCK = 512
ROPE_HALF = 64


def rope_frequencies():
    return ROPE_BASE ** (-np.arange(ROPE_HALF) / ROPE_HALF)


def rope_offsets():
    angles = np.arange(SPAN_TOKENS)[:, None] * rope_frequencies()[None, :]
    cosine, sine = np.cos(angles), np.sin(angles)
    return (
        np.concatenate([cosine, cosine], axis=1).astype(np.float32),
        np.concatenate([-sine, sine], axis=1).astype(np.float32),
    )


def rope_bases(cached):
    freqs = ROPE_BASE ** (-2.0 * jnp.arange(ROPE_HALF, dtype=jnp.float32) / (2 * ROPE_HALF))
    angles = cached.astype(jnp.float32)[:, None] * freqs[None, :]
    cosine, sine = jnp.cos(angles), jnp.sin(angles)
    return jnp.concatenate([cosine, cosine, -sine, sine], axis=1).reshape(-1, 2 * ROPE_HALF)


class Exchange:
    def __init__(self, mail, tag, pages, arrived, relays, own_sem):
        self.mail, self.tag, self.pages, self.arrived, self.relays = mail, tag, pages, arrived, relays
        self.count = pages.shape[1]
        me = ring_place(0, False)
        self.own = pltpu.make_async_copy(pages.at[me], self.slot(me, 0, self.count), own_sem)

    def slot(self, source, first, count):
        return self.arrived.at[pl.ds(source * self.count + first, count)]

    def start(self):
        half = self.count // 2
        me = ring_place(0, False)
        for flip in (False, True):
            target = self.pages.at[ring_place(2, flip)]
            f = int(flip)
            self.mail.send(
                f"{self.tag}hr{f}", target.at[:half], self.relays.at[0, f], ring_place(1, False)
            )
            self.mail.send(
                f"{self.tag}hl{f}", target.at[half:], self.relays.at[1, f], ring_place(3, False)
            )
        for name, shift, flip in (
            ("xr", 1, True),
            ("xl", 3, True),
            ("dz", 0, True),
            ("dr", 1, False),
            ("dl", 3, False),
        ):
            target = ring_place(shift, flip)
            self.mail.send(
                self.tag + name, self.pages.at[target], self.slot(me, 0, self.count), target
            )
        self.own.start()

    def relay(self):
        half = self.count // 2
        for flip in (False, True):
            f = int(flip)
            self.mail.wait(f"{self.tag}hr{f}", self.relays.at[0, f])
            self.mail.send(
                f"{self.tag}fr{f}",
                self.relays.at[0, f],
                self.slot(ring_place(3, False), 0, half),
                ring_place(1, flip),
            )
            self.mail.wait(f"{self.tag}hl{f}", self.relays.at[1, f])
            self.mail.send(
                f"{self.tag}fl{f}",
                self.relays.at[1, f],
                self.slot(ring_place(1, False), half, half),
                ring_place(3, flip),
            )

    def finish(self):
        half = self.count // 2
        self.own.wait()
        for name, shift, flip in (
            ("dr", 3, False),
            ("dl", 1, False),
            ("dz", 0, True),
            ("xr", 3, True),
            ("xl", 1, True),
        ):
            self.mail.wait(self.tag + name, self.slot(ring_place(shift, flip), 0, self.count))
        for flip in (False, True):
            f = int(flip)
            self.mail.wait(f"{self.tag}fr{f}", self.slot(ring_place(2, flip), 0, half))
            self.mail.wait(f"{self.tag}fl{f}", self.slot(ring_place(2, flip), half, half))


EXCHANGE_COPIES = 13


def layer_kernel(
    cached_ref,
    valid_ref,
    sinks_ref,
    reach_ref,
    slot_ref,
    tokens_ref,
    attn_gain_ref,
    query_gain_ref,
    key_gain_ref,
    mlp_gain_ref,
    bases_ref,
    cosine_ref,
    sine_ref,
    sink_keys_ref,
    sink_values_ref,
    pages_keys_ref,
    pages_values_ref,
    w_query_ref,
    key_weight_ref,
    value_weight_ref,
    w_headgate_ref,
    w_out_ref,
    w_gate_ref,
    w_up_ref,
    w_down_ref,
    out_ref,
    app_keys_ref,
    app_values_ref,
    w_in_vmem,
    w_headgate_vmem,
    w_out_vmem,
    w_both_vmem,
    w_down_vmem,
    rows_in,
    queries,
    near_keys,
    near_values,
    gates,
    arrived_keys,
    arrived_values,
    relay_keys,
    relay_values,
    window_rows,
    scores,
    peaks,
    weights,
    totals,
    near_sums,
    heads,
    part_one,
    part_two,
    rows_mid,
    middle,
    *rest,
):
    buffers_one, buffers_two = rest[:6], rest[6:12]
    load_sems, send_sems, recv_sems = rest[12:]
    f32, bf16 = jnp.float32, jnp.bfloat16
    units = w_down_ref.shape[0]
    head = key_weight_ref.shape[1]
    wide = w_query_ref.shape[1]
    group = wide // head
    span = SPAN_TOKENS
    query_rows = group * span
    pages = WINDOW_TOKENS // PAGE
    requests = cached_ref.shape[0]
    scale = 1.0 / math.sqrt(head)
    loads = [
        pltpu.make_async_copy(src, dst, load_sems.at[k])
        for k, (src, dst) in enumerate(
            (
                (w_query_ref, w_in_vmem.at[:, :wide]),
                (key_weight_ref, w_in_vmem.at[:, wide : wide + head]),
                (value_weight_ref, w_in_vmem.at[:, wide + head :]),
                (w_headgate_ref, w_headgate_vmem),
                (w_out_ref, w_out_vmem),
                (w_gate_ref, w_both_vmem.at[:, :units]),
                (w_up_ref, w_both_vmem.at[:, units:]),
                (w_down_ref, w_down_vmem),
            )
        )
    ]
    for load in loads:
        load.start()
    meet_neighbours()
    mail = Mailer(send_sems, recv_sems)
    plane = lax.axis_index("tp") // 4
    me = ring_place(0, False)

    def rms(values, gain):
        mean_square = jnp.mean(values * values, axis=-1, keepdims=True)
        return values * lax.rsqrt(mean_square + EPSILON) * gain

    rows_in[row_window(me, 0, ROWS), :] = rms(
        tokens_ref[...].astype(f32), attn_gain_ref[...]
    ).astype(bf16)
    gather = Gather(mail, "n", rows_in)
    gather.start()
    for member in range(requests):
        near_keys[member, span:, :] = jnp.zeros((NEAR - span, head), bf16)
        near_values[member, span:, :] = jnp.zeros((NEAR - span, head), bf16)
        sink_count = sink_keys_ref.shape[1]
        near_keys[member, span : span + sink_count, :] = sink_keys_ref[member]
        near_values[member, span : span + sink_count, :] = sink_values_ref[member]
    gather.relay_near()
    gather.relay_far()
    exchange_keys = Exchange(mail, "k", pages_keys_ref, arrived_keys, relay_keys, load_sems.at[8])
    exchange_values = Exchange(
        mail, "v", pages_values_ref, arrived_values, relay_values, load_sems.at[9]
    )
    exchange_keys.start()
    for load in loads[:4]:
        load.wait()

    def enter(flip):
        member = 1 - plane if flip else plane
        rows = pl.ds(pl.multiple_of(member * span, span), span)
        normed = rows_in[rows, :]
        mixed = jnp.dot(normed, w_in_vmem[...], preferred_element_type=f32)
        logits = jnp.dot(normed, w_headgate_vmem[...], preferred_element_type=f32)
        gates[rows, :] = 1.0 / (1.0 + jnp.exp(-logits))
        base = bases_ref[pl.ds(2 * member, 2), :]
        base_cosine, base_sine = base[0:1, :], base[1:2, :]
        cosine = base_cosine * cosine_ref[...] - base_sine * sine_ref[...]
        sine = base_sine * cosine_ref[...] + base_cosine * sine_ref[...]

        def turn(values, gain):
            normed_head = rms(values, gain)
            return (
                normed_head * cosine + pltpu.roll(normed_head, ROPE_HALF, axis=1) * sine
            ).astype(bf16)

        for part in range(group):
            queries[member, part * span : (part + 1) * span, :] = turn(
                mixed[:, part * head : (part + 1) * head], query_gain_ref[...]
            )
        fresh_keys = turn(mixed[:, wide : wide + head], key_gain_ref[...])
        fresh_values = mixed[:, wide + head :].astype(bf16)
        near_keys[member, :span, :] = fresh_keys
        near_values[member, :span, :] = fresh_values
        present = lax.broadcasted_iota(jnp.int32, (span, head), 0) < valid_ref[member]
        app_keys_ref[rows, :] = jnp.where(present, fresh_keys, jnp.zeros_like(fresh_keys))
        app_values_ref[rows, :] = jnp.where(present, fresh_values, jnp.zeros_like(fresh_values))

    enter(False)
    gather.finish()
    exchange_keys.relay()
    exchange_values.start()
    enter(True)

    def fetch(member, arrived):
        def step(index, carry):
            for part in range(8):
                page = index * 8 + part
                place = pl.ds(pl.multiple_of(page * PAGE, PAGE), PAGE)
                window_rows[place, :] = arrived[slot_ref[member * pages + page]]
            return carry

        lax.fori_loop(0, pages // 8, step, 0)

    def lane_tiles(values):
        return [values[:, k : k + 128] for k in range(0, values.shape[1], 128)]

    def score(member):
        cached, valid = cached_ref[member], valid_ref[member]
        sinks, reach = sinks_ref[member], reach_ref[member]
        contract = (((1,), (1,)), ((), ()))
        row = lax.broadcasted_iota(jnp.int32, (query_rows, NEAR), 0)
        offset = jnp.where(row >= span, row - span, row)
        column = lax.broadcasted_iota(jnp.int32, (query_rows, NEAR), 1)
        sink = column - span
        span_ok = (
            (column < valid)
            & (column <= offset)
            & ((cached + column < sinks) | (offset - column <= reach))
        )
        sink_ok = (sink < sinks) & (sink < cached - WINDOW_TOKENS)
        allowed = ((column < span) & span_ok) | (
            (column >= span) & (sink < sink_keys_ref.shape[1]) & sink_ok
        )
        near = lax.dot_general(
            queries[member], near_keys[member], contract, preferred_element_type=f32
        )
        near = jnp.where(allowed, near * scale, NEG_FILL)
        scores[:, :NEAR] = near
        peaks[...] = functools.reduce(jnp.maximum, lane_tiles(near))

        def step(index, carry):
            keys = window_rows[pl.ds(pl.multiple_of(index * BLOCK, BLOCK), BLOCK), :]
            row = lax.broadcasted_iota(jnp.int32, (query_rows, BLOCK), 0)
            offset = jnp.where(row >= span, row - span, row)
            slot = lax.broadcasted_iota(jnp.int32, (query_rows, BLOCK), 1) + index * BLOCK
            position = slot + (cached - WINDOW_TOKENS)
            allowed = (position >= 0) & (
                (position < sinks) | (WINDOW_TOKENS - slot + offset <= reach)
            )
            block = lax.dot_general(queries[member], keys, contract, preferred_element_type=f32)
            block = jnp.where(allowed, block * scale, NEG_FILL)
            scores[:, pl.ds(pl.multiple_of(NEAR + index * BLOCK, 128), BLOCK)] = block
            peaks[...] = functools.reduce(jnp.maximum, lane_tiles(block), peaks[...])
            return carry

        lax.fori_loop(0, WINDOW_TOKENS // BLOCK, step, 0)
        peak = jnp.max(peaks[...], axis=-1, keepdims=True)

        def soften(place):
            block = jnp.exp(scores[:, place] - peak)
            weights[member, :, place] = block.astype(bf16)
            return functools.reduce(jnp.add, lane_tiles(block))

        peaks[...] = soften(pl.ds(0, NEAR))

        def soft_step(index, carry):
            peaks[...] += soften(pl.ds(pl.multiple_of(NEAR + index * BLOCK, 128), BLOCK))
            return carry

        lax.fori_loop(0, WINDOW_TOKENS // BLOCK, soft_step, 0)
        totals[member] = jnp.sum(peaks[...], axis=-1, keepdims=True)
        near_sums[member] = jnp.dot(
            weights[member, :, :NEAR], near_values[member], preferred_element_type=f32
        )

    exchange_keys.finish()
    fetch(0, arrived_keys)
    score(0)
    exchange_values.relay()
    fetch(1, arrived_keys)
    score(1)
    exchange_values.finish()

    def mix(flip):
        member = 1 - plane if flip else plane
        fetch(member, arrived_values)
        summed = near_sums[member] + jnp.dot(
            weights[member, :, NEAR:], window_rows[...], preferred_element_type=f32
        )
        mixture = summed / totals[member]
        rows = pl.ds(pl.multiple_of(member * span, span), span)
        for part in range(group):
            heads[rows, part * head : (part + 1) * head] = (
                mixture[part * span : (part + 1) * span, :] * gates[rows, part : part + 1]
            ).astype(bf16)

    half_rows = 4 * ROWS

    def half(flip):
        return pl.ds(pl.multiple_of((1 - plane if flip else plane) * half_rows, half_rows), half_rows)

    scatter = Scatter(mail, "a", part_one, *buffers_one)
    loads[4].wait()

    def project(flip):
        rows = half(flip)
        part_one[rows, :] = jnp.dot(
            heads[rows, :], w_out_vmem[...], preferred_element_type=f32
        ).astype(bf16)

    mix(True)
    project(True)
    scatter.start_z()
    scatter.start_x(True)
    mix(False)
    project(False)
    scatter.start_x(False)
    scatter.relay_x(True)
    scatter.relay_x(False)
    scatter.relay_z()
    scatter.finish_relays()
    upper, lower = scatter.total()
    for first, attn in ((0, upper), (32, lower)):
        mid = tokens_ref[first : first + 32, :].astype(jnp.float32) + attn
        middle[first : first + 32, :] = mid
        mean_square = jnp.mean(mid * mid, axis=-1, keepdims=True)
        rows_mid[row_window(me, first, 32), :] = (
            mid * lax.rsqrt(mean_square + EPSILON) * mlp_gain_ref[...]
        ).astype(jnp.bfloat16)
    gather = Gather(mail, "g", rows_mid)
    gather.start()
    gather.relay_near()
    for load in loads[5:]:
        load.wait()

    def feed(flip):
        rows = half(flip)
        both = jnp.dot(rows_mid[rows, :], w_both_vmem[...], preferred_element_type=jnp.float32)
        gate, up = both[:, :units], both[:, units:]
        hidden = (gate / (1.0 + jnp.exp(-gate)) * up).astype(jnp.bfloat16)
        part_two[rows, :] = jnp.dot(
            hidden, w_down_vmem[...], preferred_element_type=jnp.float32
        ).astype(jnp.bfloat16)

    scatter = Scatter(mail, "b", part_two, *buffers_two)
    gather.relay_far()
    feed(False)
    scatter.start_x(False)
    gather.finish()
    feed(True)
    scatter.start_z()
    scatter.start_x(True)
    scatter.relay_x(False)
    scatter.relay_x(True)
    scatter.relay_z()
    scatter.finish_relays()
    upper, lower = scatter.total()
    out_ref[0:32, :] = middle[0:32, :] + upper
    out_ref[32:64, :] = middle[32:64, :] + lower
    mail.drain()


def layer(
    tokens,
    attn_gain,
    query_gain,
    key_gain,
    mlp_gain,
    sink_keys,
    sink_values,
    pages_keys,
    pages_values,
    w_query,
    key_weight,
    value_weight,
    w_headgate,
    w_out,
    w_gate,
    w_up,
    w_down,
    cached,
    valid,
    sinks,
    reach,
    slots,
):
    bf16, f32 = jnp.bfloat16, jnp.float32
    requests, _, head = sink_keys.shape
    rows_total = requests * SPAN_TOKENS
    group = w_query.shape[1] // head
    query_rows = group * SPAN_TOKENS
    smem = pl.BlockSpec(memory_space=pltpu.SMEM)
    vmem = pl.BlockSpec(memory_space=pltpu.VMEM)
    hbm = pl.BlockSpec(memory_space=pl.ANY)
    arrived = (pages_keys.shape[0] * pages_keys.shape[1], PAGE, head)
    relays = (2, 2, pages_keys.shape[1] // 2, PAGE, head)
    buffers = [pltpu.VMEM(shape, bf16) for shape in SCATTER_BUFFERS]
    copies = 2 * (SCATTER_COPIES + GATHER_COPIES + EXCHANGE_COPIES)
    cosine, sine = rope_offsets()
    return pl.pallas_call(
        layer_kernel,
        out_shape=(
            jax.ShapeDtypeStruct(tokens.shape, f32),
            jax.ShapeDtypeStruct((rows_total, head), bf16),
            jax.ShapeDtypeStruct((rows_total, head), bf16),
        ),
        in_specs=[smem] * 5 + [vmem] * 10 + [hbm] * 10,
        out_specs=(vmem, vmem, vmem),
        scratch_shapes=[
            pltpu.VMEM((w_query.shape[0], (group + 2) * head), bf16),
            pltpu.VMEM(w_headgate.shape, bf16),
            pltpu.VMEM(w_out.shape, bf16),
            pltpu.VMEM((w_gate.shape[0], 2 * w_gate.shape[1]), bf16),
            pltpu.VMEM(w_down.shape, bf16),
            pltpu.VMEM((rows_total, WIDTH), bf16),
            pltpu.VMEM((requests, query_rows, head), bf16),
            pltpu.VMEM((requests, NEAR, head), bf16),
            pltpu.VMEM((requests, NEAR, head), bf16),
            pltpu.VMEM((rows_total, w_headgate.shape[1]), f32),
            pltpu.VMEM(arrived, bf16),
            pltpu.VMEM(arrived, bf16),
            pltpu.VMEM(relays, bf16),
            pltpu.VMEM(relays, bf16),
            pltpu.VMEM((WINDOW_TOKENS, head), bf16),
            pltpu.VMEM((query_rows, NEAR + WINDOW_TOKENS), f32),
            pltpu.VMEM((query_rows, 128), f32),
            pltpu.VMEM((requests, query_rows, NEAR + WINDOW_TOKENS), bf16),
            pltpu.VMEM((requests, query_rows, 1), f32),
            pltpu.VMEM((requests, query_rows, head), f32),
            pltpu.VMEM((rows_total, group * head), bf16),
            pltpu.VMEM((rows_total, WIDTH), bf16),
            pltpu.VMEM((rows_total, WIDTH), bf16),
            pltpu.VMEM((rows_total, WIDTH), bf16),
            pltpu.VMEM(tokens.shape, f32),
            *buffers,
            *buffers,
            pltpu.SemaphoreType.DMA((10,)),
            pltpu.SemaphoreType.DMA((copies,)),
            pltpu.SemaphoreType.DMA((copies,)),
        ],
        compiler_params=pltpu.CompilerParams(
            collective_id=1, has_side_effects=True, vmem_limit_bytes=63 * 1024 * 1024
        ),
        name="layer",
    )(
        cached,
        valid,
        sinks,
        reach,
        slots,
        tokens,
        attn_gain[None, :],
        query_gain[None, :],
        key_gain[None, :],
        mlp_gain[None, :],
        rope_bases(cached),
        jnp.asarray(cosine),
        jnp.asarray(sine),
        sink_keys,
        sink_values,
        pages_keys,
        pages_values,
        w_query,
        key_weight,
        value_weight,
        w_headgate,
        w_out,
        w_gate,
        w_up,
        w_down,
    )


def body(
    tokens,
    attn_gain,
    w_query,
    key_weight,
    value_weight,
    w_headgate,
    query_gain,
    key_gain,
    w_out,
    mlp_gain,
    w_gate,
    w_up,
    w_down,
    pooled_keys,
    pooled_values,
    sink_key_cache,
    sink_value_cache,
    cached_length,
    valid_length,
    sink_position_count,
    window,
    page_slot,
):
    head_dim = query_gain.shape[0]

    def by_head(pool):
        return pool.transpose(2, 0, 1, 3)

    output, app_keys, app_values = layer(
        tokens,
        attn_gain,
        query_gain,
        key_gain,
        mlp_gain,
        sink_key_cache[:, :, 0, :],
        sink_value_cache[:, :, 0, :],
        by_head(pooled_keys),
        by_head(pooled_values),
        w_query,
        key_weight,
        value_weight,
        jnp.pad(w_headgate, ((0, 0), (0, 128 - w_headgate.shape[1]))),
        w_out,
        w_gate,
        w_up,
        w_down,
        cached_length,
        valid_length,
        sink_position_count,
        window,
        page_slot[0],
    )
    return (output, app_keys[:, None, :], app_values[:, None, :])


def solution(mesh):
    in_specs = (
        P(("req", "tp"), None),
        P(),
        P(None, "tp"),
        P(None, "tp"),
        P(None, "tp"),
        P(None, "tp"),
        P(),
        P(),
        P("tp", None),
        P(),
        P(None, "tp"),
        P(None, "tp"),
        P("tp", None),
        P(("req", "tp"), None, None, None),
        P(("req", "tp"), None, None, None),
        P("req", None, "tp", None),
        P("req", None, "tp", None),
        P("req"),
        P("req"),
        P("req"),
        P("req"),
        P("req", None),
    )
    out_specs = (P(("req", "tp"), None), P("req", "tp", None), P("req", "tp", None))
    return jax.shard_map(body, mesh=mesh, in_specs=in_specs, out_specs=out_specs, check_vma=False)
```

```python
import functools
import math

import jax
import jax.numpy as jnp
import numpy as np
from jax import lax
from jax.experimental import pallas as pl
from jax.experimental.pallas import tpu as pltpu
from jax.sharding import PartitionSpec as P

WINDOW_TOKENS = 4096
SPAN_TOKENS = 256


EPSILON = 1e-06
ROPE_BASE = 1000000.0
NEG_FILL = -1e30

MESH = pl.DeviceIdType.MESH
ROWS = 64
WIDTH = 2048
PEERS = ((1, False), (3, False), (0, True), (1, True), (3, True))
CORES = 2
Z_GROUPS = 4


def ring_place(shift, flip):
    t = lax.axis_index("tp")
    x = lax.rem(t, 4)
    z = t // 4
    plane = 1 - z if flip else z
    return lax.rem(x + shift, 4) + 4 * plane


def beyond_place():
    req = lax.axis_index("req")
    t = lax.axis_index("tp")
    group = req // CORES
    z_group = lax.rem(group, Z_GROUPS)
    step = jnp.where(t // 4 == 1, 1, Z_GROUPS - 1)
    moved = group - z_group + lax.rem(z_group + step, Z_GROUPS)
    return {"req": moved * CORES + lax.rem(req, CORES), "tp": ring_place(0, True)}


def row_window(owner, first, count):
    return pl.ds(pl.multiple_of(owner * ROWS + first, 16), count)


class Mailer:
    def __init__(self, send_sems, recv_sems):
        self.send_sems, self.recv_sems = send_sems, recv_sems
        self.slots = {}
        self.sent = []

    def slot(self, name):
        return self.slots.setdefault(name, len(self.slots))

    def send(self, name, src, dst, target):
        k = self.slot(name)
        copy = pltpu.make_async_remote_copy(
            src_ref=src,
            dst_ref=dst,
            send_sem=self.send_sems.at[k],
            recv_sem=self.recv_sems.at[k],
            device_id=target if isinstance(target, dict) else {"tp": target},
            device_id_type=MESH,
        )
        copy.start()
        self.sent.append(copy)

    def wait(self, name, dst):
        k = self.slot(name)
        pltpu.make_async_remote_copy(
            src_ref=dst,
            dst_ref=dst,
            send_sem=self.send_sems.at[k],
            recv_sem=self.recv_sems.at[k],
            device_id={"tp": ring_place(0, True)},
            device_id_type=MESH,
        ).wait_recv()

    def drain(self):
        for copy in self.sent:
            copy.wait_send()
        self.sent = []


def meet_neighbours():
    barrier = pltpu.get_barrier_semaphore()
    for shift, flip in PEERS:
        pl.semaphore_signal(
            barrier, inc=1, device_id={"tp": ring_place(shift, flip)}, device_id_type=MESH
        )
    pl.semaphore_signal(barrier, inc=1, device_id=beyond_place(), device_id_type=MESH)
    pl.semaphore_wait(barrier, len(PEERS) + 1)


def add_into(part, owner, first, count, arrived):
    rows = row_window(owner, first, count)
    part[rows, :] = (
        part[rows, :].astype(jnp.float32) + arrived[...].astype(jnp.float32)
    ).astype(jnp.bfloat16)


class Scatter:
    def __init__(self, mail, tag, part, h1, h2, zb, b1, b2, za):
        self.mail, self.tag, self.part = mail, tag, part
        self.h1, self.h2, self.zb, self.b1, self.b2, self.za = h1, h2, zb, b1, b2, za
        self.right, self.left, self.across = ring_place(1, False), ring_place(3, False), ring_place(0, True)

    def rows(self, shift, flip, first, count):
        return self.part.at[row_window(ring_place(shift, flip), first, count), :]

    def put(self, name, src, dst, target):
        self.mail.send(self.tag + name, src, dst, target)

    def got(self, name, dst):
        self.mail.wait(self.tag + name, dst)

    def start_x(self, flip):
        f = int(flip)
        self.put(f"h1r{f}", self.rows(2, flip, 0, 16), self.h1.at[0, f], self.right)
        self.put(f"h1l{f}", self.rows(2, flip, 16, 16), self.h1.at[1, f], self.left)
        self.put(f"h2r{f}1", self.rows(1, flip, 16, 16), self.h2.at[0, f, 1], self.right)
        self.put(f"h2l{f}0", self.rows(3, flip, 0, 16), self.h2.at[1, f, 0], self.left)

    def start_z(self):
        for k, shift in enumerate((2, 1, 3)):
            self.put(f"zb{k}", self.rows(shift, True, 32, 32), self.zb.at[k], self.across)

    def relay_x(self, flip):
        f = int(flip)
        self.got(f"h1r{f}", self.h1.at[0, f])
        add_into(self.part, ring_place(1, flip), 0, 16, self.h1.at[0, f])
        self.put(f"h2r{f}0", self.rows(1, flip, 0, 16), self.h2.at[0, f, 0], self.right)
        self.got(f"h1l{f}", self.h1.at[1, f])
        add_into(self.part, ring_place(3, flip), 16, 16, self.h1.at[1, f])
        self.put(f"h2l{f}1", self.rows(3, flip, 16, 16), self.h2.at[1, f, 1], self.left)

    def relay_z(self):
        self.got("zb0", self.zb.at[0])
        add_into(self.part, ring_place(2, False), 32, 32, self.zb.at[0])
        self.put("b1r", self.rows(2, False, 32, 16), self.b1.at[0], self.right)
        self.put("b1l", self.rows(2, False, 48, 16), self.b1.at[1], self.left)
        self.got("zb1", self.zb.at[1])
        add_into(self.part, ring_place(1, False), 32, 32, self.zb.at[1])
        self.put("b2r1", self.rows(1, False, 48, 16), self.b2.at[0, 1], self.right)
        self.got("zb2", self.zb.at[2])
        add_into(self.part, ring_place(3, False), 32, 32, self.zb.at[2])
        self.put("b2l0", self.rows(3, False, 32, 16), self.b2.at[1, 0], self.left)

    def cross(self):
        for side, letter in ((0, "r"), (1, "l")):
            for half in (0, 1):
                self.got(f"h2{letter}1{half}", self.h2.at[side, 1, half])
        rows = row_window(self.across, 0, 32)
        self.part[rows, :] = (
            self.part[rows, :].astype(jnp.float32)
            + self.h2[0, 1].reshape(32, WIDTH).astype(jnp.float32)
            + self.h2[1, 1].reshape(32, WIDTH).astype(jnp.float32)
        ).astype(jnp.bfloat16)
        self.put("za", self.rows(0, True, 0, 32), self.za, self.across)
        self.put("zb3", self.rows(0, True, 32, 32), self.zb.at[3], self.across)

    def finish_relays(self):
        self.got("b1r", self.b1.at[0])
        add_into(self.part, ring_place(1, False), 32, 16, self.b1.at[0])
        self.put("b2r0", self.rows(1, False, 32, 16), self.b2.at[0, 0], self.right)
        self.got("b1l", self.b1.at[1])
        add_into(self.part, ring_place(3, False), 48, 16, self.b1.at[1])
        self.put("b2l1", self.rows(3, False, 48, 16), self.b2.at[1, 1], self.left)

    def upper(self):
        f32 = jnp.float32
        for side, letter in ((0, "r"), (1, "l")):
            for half in (0, 1):
                self.got(f"h2{letter}0{half}", self.h2.at[side, 0, half])
        upper = (
            self.part[row_window(ring_place(0, False), 0, 32), :].astype(f32)
            + self.h2[0, 0].reshape(32, WIDTH).astype(f32)
            + self.h2[1, 0].reshape(32, WIDTH).astype(f32)
        )
        self.got("za", self.za)
        return upper + self.za[...].astype(f32)

    def lower(self):
        f32 = jnp.float32
        for side, letter in ((0, "r"), (1, "l")):
            for half in (0, 1):
                self.got(f"b2{letter}{half}", self.b2.at[side, half])
        self.got("zb3", self.zb.at[3])
        return (
            self.part[row_window(ring_place(0, False), 32, 32), :].astype(f32)
            + self.b2[0].reshape(32, WIDTH).astype(f32)
            + self.b2[1].reshape(32, WIDTH).astype(f32)
            + self.zb[3].astype(f32)
        )


SCATTER_BUFFERS = [
    ((2, 2, 16, WIDTH)),
    ((2, 2, 2, 16, WIDTH)),
    ((4, 32, WIDTH)),
    ((2, 16, WIDTH)),
    ((2, 2, 16, WIDTH)),
    ((32, WIDTH)),
]
SCATTER_COPIES = 24


class Gather:
    def __init__(self, mail, tag, rows):
        self.mail, self.tag, self.rows = mail, tag, rows
        self.right, self.left, self.across = ring_place(1, False), ring_place(3, False), ring_place(0, True)

    def part(self, shift, flip, first, count):
        return self.rows.at[row_window(ring_place(shift, flip), first, count), :]

    def put(self, name, place, target):
        ref = self.part(*place)
        self.mail.send(self.tag + name, ref, ref, target)

    def got(self, name, place):
        self.mail.wait(self.tag + name, self.part(*place))

    def start(self):
        self.put("z0", (0, False, 0, 32), self.across)
        self.put("r0", (0, False, 32, 32), self.right)
        self.put("l0", (0, False, 32, 32), self.left)
        self.put("r1", (0, False, 0, 32), self.right)
        self.put("l1", (0, False, 0, 32), self.left)
        self.put("z1", (0, False, 32, 32), self.across)

    def relay_near(self):
        self.got("r0", (3, False, 32, 32))
        self.put("r2", (3, False, 32, 16), self.right)
        self.put("z2", (3, False, 32, 32), self.across)
        self.got("l0", (1, False, 32, 32))
        self.put("l2", (1, False, 48, 16), self.left)
        self.put("z3", (1, False, 32, 32), self.across)
        self.got("r1", (3, False, 0, 32))
        self.put("r4", (3, False, 0, 16), self.right)
        self.got("l1", (1, False, 0, 32))
        self.put("l4", (1, False, 16, 16), self.left)
        self.got("z0", (0, True, 0, 32))
        self.put("r3", (0, True, 0, 32), self.right)
        self.put("l3", (0, True, 0, 32), self.left)
        self.got("r2", (2, False, 32, 16))
        self.put("z4", (2, False, 32, 16), self.across)
        self.got("l2", (2, False, 48, 16))
        self.put("z5", (2, False, 48, 16), self.across)
        self.got("r4", (2, False, 0, 16))
        self.got("l4", (2, False, 16, 16))

    def relay_far(self):
        self.got("r3", (3, True, 0, 32))
        self.put("r5", (3, True, 0, 16), self.right)
        self.got("l3", (1, True, 0, 32))
        self.put("l5", (1, True, 16, 16), self.left)

    def finish(self):
        self.got("r5", (2, True, 0, 16))
        self.got("l5", (2, True, 16, 16))
        self.got("z1", (0, True, 32, 32))
        self.got("z2", (3, True, 32, 32))
        self.got("z3", (1, True, 32, 32))
        self.got("z4", (2, True, 32, 16))
        self.got("z5", (2, True, 48, 16))


GATHER_COPIES = 18
OWN_ROWS = 4 * ROWS
HALF = ROWS // 2


def x_place(shift):
    return lax.rem(lax.axis_index("tp") + shift, 4)


def wide_window(block, shift, half=None):
    x = x_place(shift)
    if block == 0:
        return pl.ds(pl.multiple_of(x * ROWS + (half or 0) * HALF, HALF), ROWS if half is None else HALF)
    return pl.ds(pl.multiple_of(OWN_ROWS + (block - 1) * 4 * HALF + x * HALF, HALF), HALF)


class WideGather:
    def __init__(self, mail, rows):
        self.mail, self.rows = mail, rows
        self.right, self.left = ring_place(1, False), ring_place(3, False)
        self.over = (ring_place(0, True), beyond_place())

    def put(self, name, shift, half, block, target):
        self.mail.send(
            "w" + name,
            self.rows.at[wide_window(0, shift, half), :],
            self.rows.at[wide_window(block, shift, half), :],
            target,
        )

    def got(self, name, shift, half, block):
        self.mail.wait("w" + name, self.rows.at[wide_window(block, shift, half), :])

    def start(self, half):
        self.put(f"r{half}", 0, half, 0, self.right)
        self.put(f"l{half}", 0, half, 0, self.left)
        self.put(f"z{half}0", 0, half, half + 1, self.over[half])

    def relay(self):
        for half in (0, 1):
            self.got(f"r{half}", 3, half, 0)
            if half == 0:
                self.put("rr", 3, half, 0, self.right)
            self.put(f"z{half}3", 3, half, half + 1, self.over[half])
            self.got(f"l{half}", 1, half, 0)
            if half == 1:
                self.put("ll", 1, half, 0, self.left)
            self.put(f"z{half}1", 1, half, half + 1, self.over[half])
        self.got("rr", 2, 0, 0)
        self.put("z02", 2, 0, 1, self.over[0])
        self.got("ll", 2, 1, 0)
        self.put("z12", 2, 1, 2, self.over[1])

    def finish(self, half):
        for shift in (0, 3, 1, 2):
            self.got(f"z{half}{shift}", shift, half, half + 1)


WIDE_GATHER_COPIES = 14


class WideScatter:
    def __init__(self, mail, part, arrived, hop_one, hop_two):
        self.mail, self.part, self.arrived = mail, part, arrived
        self.hop_one, self.hop_two = hop_one, hop_two
        self.right, self.left = ring_place(1, False), ring_place(3, False)
        self.over = (ring_place(0, True), beyond_place())

    def start(self, half):
        for k, shift in enumerate((2, 1, 3, 0)):
            self.mail.send(
                f"y{half}{k}",
                self.part.at[wide_window(half + 1, shift), :],
                self.arrived.at[half, k],
                self.over[half],
            )

    def fold(self, half, k, shift):
        self.mail.wait(f"y{half}{k}", self.arrived.at[half, k])
        self.add(shift, half, self.arrived[half, k])

    def add(self, shift, half, values):
        rows = wide_window(0, shift, half)
        self.part[rows, :] = (
            self.part[rows, :].astype(jnp.float32) + values.astype(jnp.float32)
        ).astype(jnp.bfloat16)

    def put(self, name, shift, half, dst, target):
        self.mail.send("y" + name, self.part.at[wide_window(0, shift, half), :], dst, target)

    def relay(self):
        self.fold(0, 0, 2)
        self.put("hr", 2, 0, self.hop_one.at[0], self.right)
        self.fold(1, 0, 2)
        self.put("hl", 2, 1, self.hop_one.at[1], self.left)
        self.fold(1, 1, 1)
        self.put("r1", 1, 1, self.hop_two.at[0, 1], self.right)
        self.fold(0, 1, 1)
        self.mail.wait("yhr", self.hop_one.at[0])
        self.add(1, 0, self.hop_one[0])
        self.put("r0", 1, 0, self.hop_two.at[0, 0], self.right)
        self.fold(0, 2, 3)
        self.put("l0", 3, 0, self.hop_two.at[1, 0], self.left)
        self.fold(1, 2, 3)
        self.mail.wait("yhl", self.hop_one.at[1])
        self.add(3, 1, self.hop_one[1])
        self.put("l1", 3, 1, self.hop_two.at[1, 1], self.left)

    def total(self, half):
        f32 = jnp.float32
        self.mail.wait(f"y{half}3", self.arrived.at[half, 3])
        self.mail.wait(f"yr{half}", self.hop_two.at[0, half])
        self.mail.wait(f"yl{half}", self.hop_two.at[1, half])
        return (
            self.part[wide_window(0, 0, half), :].astype(f32)
            + self.arrived[half, 3].astype(f32)
            + self.hop_two[0, half].astype(f32)
            + self.hop_two[1, half].astype(f32)
        )


WIDE_BUFFERS = [(2, 4, HALF, WIDTH), (2, HALF, WIDTH), (2, 2, HALF, WIDTH)]
WIDE_SCATTER_COPIES = 14


PAGE = 16
NEAR = 384
BLOCK = 512
ROPE_HALF = 64


def rope_frequencies():
    return ROPE_BASE ** (-np.arange(ROPE_HALF) / ROPE_HALF)


def rope_offsets():
    angles = np.arange(SPAN_TOKENS)[:, None] * rope_frequencies()[None, :]
    cosine, sine = np.cos(angles), np.sin(angles)
    return (
        np.concatenate([cosine, cosine], axis=1).astype(np.float32),
        np.concatenate([-sine, sine], axis=1).astype(np.float32),
    )


class Exchange:
    def __init__(self, mail, tag, pages, arrived, relays, own_sem):
        self.mail, self.tag, self.pages, self.arrived, self.relays = mail, tag, pages, arrived, relays
        self.count = pages.shape[1]
        me = ring_place(0, False)
        self.own = pltpu.make_async_copy(pages.at[me], self.slot(me, 0, self.count), own_sem)

    def slot(self, source, first, count):
        return self.arrived.at[pl.ds(source * self.count + first, count)]

    def start(self):
        half = self.count // 2
        me = ring_place(0, False)
        for flip in (False, True):
            target = self.pages.at[ring_place(2, flip)]
            f = int(flip)
            self.mail.send(
                f"{self.tag}hr{f}", target.at[:half], self.relays.at[0, f], ring_place(1, False)
            )
            self.mail.send(
                f"{self.tag}hl{f}", target.at[half:], self.relays.at[1, f], ring_place(3, False)
            )
        for name, shift, flip in (
            ("xr", 1, True),
            ("xl", 3, True),
            ("dz", 0, True),
            ("dr", 1, False),
            ("dl", 3, False),
        ):
            target = ring_place(shift, flip)
            self.mail.send(
                self.tag + name, self.pages.at[target], self.slot(me, 0, self.count), target
            )
        self.own.start()

    def relay(self):
        half = self.count // 2
        for flip in (False, True):
            f = int(flip)
            self.mail.wait(f"{self.tag}hr{f}", self.relays.at[0, f])
            self.mail.send(
                f"{self.tag}fr{f}",
                self.relays.at[0, f],
                self.slot(ring_place(3, False), 0, half),
                ring_place(1, flip),
            )
            self.mail.wait(f"{self.tag}hl{f}", self.relays.at[1, f])
            self.mail.send(
                f"{self.tag}fl{f}",
                self.relays.at[1, f],
                self.slot(ring_place(1, False), half, half),
                ring_place(3, flip),
            )

    def finish(self):
        half = self.count // 2
        self.own.wait()
        for name, shift, flip in (
            ("dr", 3, False),
            ("dl", 1, False),
            ("dz", 0, True),
            ("xr", 3, True),
            ("xl", 1, True),
        ):
            self.mail.wait(self.tag + name, self.slot(ring_place(shift, flip), 0, self.count))
        for flip in (False, True):
            f = int(flip)
            self.mail.wait(f"{self.tag}fr{f}", self.slot(ring_place(2, flip), 0, half))
            self.mail.wait(f"{self.tag}fl{f}", self.slot(ring_place(2, flip), half, half))


EXCHANGE_COPIES = 13


def layer_kernel(
    cached_ref,
    valid_ref,
    sinks_ref,
    reach_ref,
    slot_ref,
    tokens_ref,
    attn_gain_ref,
    query_gain_ref,
    key_gain_ref,
    mlp_gain_ref,
    freqs_ref,
    cosine_ref,
    sine_ref,
    sink_keys_ref,
    sink_values_ref,
    pages_keys_ref,
    pages_values_ref,
    w_query_ref,
    key_weight_ref,
    value_weight_ref,
    w_headgate_ref,
    w_out_ref,
    w_gate_ref,
    w_up_ref,
    w_down_ref,
    out_ref,
    fresh_keys_ref,
    fresh_values_ref,
    w_in_vmem,
    w_headgate_vmem,
    w_out_vmem,
    w_both_vmem,
    w_down_vmem,
    rows_in,
    queries,
    near_keys,
    near_values,
    gates,
    arrived_keys,
    arrived_values,
    raw_pages,
    head_keys,
    head_values,
    relay_keys,
    relay_values,
    window_rows,
    scores,
    peaks,
    weights,
    totals,
    near_sums,
    heads,
    part_one,
    part_two,
    rows_mid,
    middle,
    *rest,
):
    buffers_one, buffers_two = rest[:6], rest[6:9]
    load_sems, send_sems, recv_sems = rest[9:]
    f32, bf16 = jnp.float32, jnp.bfloat16
    units = w_down_ref.shape[0]
    head = key_weight_ref.shape[1]
    query_width = w_query_ref.shape[1]
    group = query_width // head
    span = SPAN_TOKENS
    query_rows = group * span
    pages = WINDOW_TOKENS // PAGE
    requests = cached_ref.shape[0]
    scale = 1.0 / math.sqrt(head)
    loads = [
        pltpu.make_async_copy(src, dst, load_sems.at[k])
        for k, (src, dst) in enumerate(
            (
                (w_query_ref, w_in_vmem.at[:, :query_width]),
                (key_weight_ref, w_in_vmem.at[:, query_width : query_width + head]),
                (value_weight_ref, w_in_vmem.at[:, query_width + head :]),
                (w_headgate_ref, w_headgate_vmem),
                (w_out_ref, w_out_vmem),
                (w_gate_ref, w_both_vmem.at[:, :units]),
                (w_up_ref, w_both_vmem.at[:, units:]),
                (w_down_ref, w_down_vmem),
            )
        )
    ]
    raw_loads = [
        pltpu.make_async_copy(pages_keys_ref, raw_pages.at[0], load_sems.at[10]),
        pltpu.make_async_copy(pages_values_ref, raw_pages.at[1], load_sems.at[11]),
    ]
    for load in raw_loads + loads:
        load.start()
    meet_neighbours()
    mail = Mailer(send_sems, recv_sems)
    plane = lax.axis_index("tp") // 4
    me = ring_place(0, False)

    def rms(values, gain):
        mean_square = jnp.mean(values * values, axis=-1, keepdims=True)
        return values * lax.rsqrt(mean_square + EPSILON) * gain

    rows_in[row_window(me, 0, ROWS), :] = rms(
        tokens_ref[...].astype(f32), attn_gain_ref[...]
    ).astype(bf16)
    gather = Gather(mail, "n", rows_in)
    gather.start()
    for member in range(requests):
        near_keys[member, span:, :] = jnp.zeros((NEAR - span, head), bf16)
        near_values[member, span:, :] = jnp.zeros((NEAR - span, head), bf16)
        sink_count = sink_keys_ref.shape[1]
        near_keys[member, span : span + sink_count, :] = sink_keys_ref[member]
        near_values[member, span : span + sink_count, :] = sink_values_ref[member]

    def by_head(which, target):
        raw_loads[which].wait()
        count = 8

        def step(index, carry):
            place = pl.ds(index * count, count)
            block = raw_pages[which, place].reshape(count * PAGE, *raw_pages.shape[3:])
            target[:, place] = jnp.swapaxes(block, 0, 1).reshape(-1, count, PAGE, head)
            return carry

        lax.fori_loop(0, raw_pages.shape[1] // count, step, 0)

    by_head(0, head_keys)
    gather.relay_near()
    gather.relay_far()
    exchange_keys = Exchange(mail, "k", head_keys, arrived_keys, relay_keys, load_sems.at[8])
    exchange_values = Exchange(
        mail, "v", head_values, arrived_values, relay_values, load_sems.at[9]
    )
    exchange_keys.start()
    for load in loads[:4]:
        load.wait()

    def enter(flip):
        member = 1 - plane if flip else plane
        rows = pl.ds(pl.multiple_of(member * span, span), span)
        normed = rows_in[rows, :]
        mixed = jnp.dot(normed, w_in_vmem[...], preferred_element_type=f32)
        logits = lax.dot_general(
            normed, w_headgate_vmem[...], (((1,), (1,)), ((), ())), preferred_element_type=f32
        )
        gates[rows, :] = 1.0 / (1.0 + jnp.exp(-logits))
        angles = cached_ref[member].astype(f32) * freqs_ref[...]
        lanes = lax.broadcasted_iota(jnp.int32, angles.shape, 1)
        base_cosine = jnp.cos(angles)
        base_sine = jnp.where(lanes < ROPE_HALF, -jnp.sin(angles), jnp.sin(angles))
        cosine = base_cosine * cosine_ref[...] - base_sine * sine_ref[...]
        sine = base_sine * cosine_ref[...] + base_cosine * sine_ref[...]

        def turn(values, gain):
            normed_head = rms(values, gain)
            return (
                normed_head * cosine + pltpu.roll(normed_head, ROPE_HALF, axis=1) * sine
            ).astype(bf16)

        for part in range(group):
            queries[member, part * span : (part + 1) * span, :] = turn(
                mixed[:, part * head : (part + 1) * head], query_gain_ref[...]
            )
        fresh_keys = turn(mixed[:, query_width : query_width + head], key_gain_ref[...])
        fresh_values = mixed[:, query_width + head :].astype(bf16)
        near_keys[member, :span, :] = fresh_keys
        near_values[member, :span, :] = fresh_values
        fresh_keys_ref[rows, :] = fresh_keys
        fresh_values_ref[rows, :] = fresh_values

    by_head(1, head_values)
    enter(False)
    gather.finish()
    exchange_keys.relay()
    exchange_values.start()
    enter(True)

    def fetch(member, arrived):
        def step(index, carry):
            for part in range(8):
                page = index * 8 + part
                place = pl.ds(pl.multiple_of(page * PAGE, PAGE), PAGE)
                window_rows[place, :] = arrived[slot_ref[member * pages + page]]
            return carry

        lax.fori_loop(0, pages // 8, step, 0)

    def lane_tiles(values):
        return [values[:, k : k + 128] for k in range(0, values.shape[1], 128)]

    def score(member):
        cached, valid = cached_ref[member], valid_ref[member]
        sinks, reach = sinks_ref[member], reach_ref[member]
        contract = (((1,), (1,)), ((), ()))
        row = lax.broadcasted_iota(jnp.int32, (query_rows, NEAR), 0)
        offset = jnp.where(row >= span, row - span, row)
        column = lax.broadcasted_iota(jnp.int32, (query_rows, NEAR), 1)
        sink = column - span
        span_ok = (
            (column < valid)
            & (column <= offset)
            & ((cached + column < sinks) | (offset - column <= reach))
        )
        sink_ok = (sink < sinks) & (sink < cached - WINDOW_TOKENS)
        allowed = ((column < span) & span_ok) | (
            (column >= span) & (sink < sink_keys_ref.shape[1]) & sink_ok
        )
        near = lax.dot_general(
            queries[member], near_keys[member], contract, preferred_element_type=f32
        )
        near = jnp.where(allowed, near * scale, NEG_FILL)
        scores[:, :NEAR] = near
        peaks[...] = functools.reduce(jnp.maximum, lane_tiles(near))

        def step(index, carry):
            keys = window_rows[pl.ds(pl.multiple_of(index * BLOCK, BLOCK), BLOCK), :]
            row = lax.broadcasted_iota(jnp.int32, (query_rows, BLOCK), 0)
            offset = jnp.where(row >= span, row - span, row)
            slot = lax.broadcasted_iota(jnp.int32, (query_rows, BLOCK), 1) + index * BLOCK
            position = slot + (cached - WINDOW_TOKENS)
            allowed = (position >= 0) & (
                (position < sinks) | (WINDOW_TOKENS - slot + offset <= reach)
            )
            block = lax.dot_general(queries[member], keys, contract, preferred_element_type=f32)
            block = jnp.where(allowed, block * scale, NEG_FILL)
            scores[:, pl.ds(pl.multiple_of(NEAR + index * BLOCK, 128), BLOCK)] = block
            peaks[...] = functools.reduce(jnp.maximum, lane_tiles(block), peaks[...])
            return carry

        lax.fori_loop(0, WINDOW_TOKENS // BLOCK, step, 0)
        peak = jnp.max(peaks[...], axis=-1, keepdims=True)

        def soften(place):
            block = jnp.exp(scores[:, place] - peak)
            weights[member, :, place] = block.astype(bf16)
            return functools.reduce(jnp.add, lane_tiles(block))

        peaks[...] = soften(pl.ds(0, NEAR))

        def soft_step(index, carry):
            peaks[...] += soften(pl.ds(pl.multiple_of(NEAR + index * BLOCK, 128), BLOCK))
            return carry

        lax.fori_loop(0, WINDOW_TOKENS // BLOCK, soft_step, 0)
        totals[member] = jnp.sum(peaks[...], axis=-1, keepdims=True)
        near_sums[member] = jnp.dot(
            weights[member, :, :NEAR], near_values[member], preferred_element_type=f32
        )

    exchange_keys.finish()
    fetch(0, arrived_keys)
    score(0)
    exchange_values.relay()
    fetch(1, arrived_keys)
    score(1)
    exchange_values.finish()

    def mix(flip):
        member = 1 - plane if flip else plane
        fetch(member, arrived_values)
        summed = near_sums[member] + jnp.dot(
            weights[member, :, NEAR:], window_rows[...], preferred_element_type=f32
        )
        mixture = summed / totals[member]
        rows = pl.ds(pl.multiple_of(member * span, span), span)
        for part in range(group):
            heads[rows, part * head : (part + 1) * head] = (
                mixture[part * span : (part + 1) * span, :] * gates[rows, part : part + 1]
            ).astype(bf16)

    half_rows = 4 * ROWS

    def half(flip):
        return pl.ds(pl.multiple_of((1 - plane if flip else plane) * half_rows, half_rows), half_rows)

    scatter = Scatter(mail, "a", part_one, *buffers_one)
    loads[4].wait()

    def project(flip):
        rows = half(flip)
        part_one[rows, :] = jnp.dot(
            heads[rows, :], w_out_vmem[...], preferred_element_type=f32
        ).astype(bf16)

    mix(True)
    project(True)
    scatter.start_z()
    scatter.start_x(True)
    mix(False)
    project(False)
    scatter.start_x(False)
    scatter.relay_x(True)
    scatter.relay_x(False)
    scatter.cross()
    scatter.relay_z()
    scatter.finish_relays()
    wide = WideGather(mail, rows_mid)

    def settle(half_index, attn):
        first = half_index * HALF
        mid = tokens_ref[first : first + HALF, :].astype(f32) + attn
        middle[first : first + HALF, :] = mid
        rows_mid[wide_window(0, 0, half_index), :] = rms(mid, mlp_gain_ref[...]).astype(bf16)
        wide.start(half_index)

    settle(0, scatter.upper())
    settle(1, scatter.lower())
    wide.relay()
    for load in loads[5:]:
        load.wait()

    def feed(first, count):
        both = jnp.dot(
            rows_mid[first : first + count, :], w_both_vmem[...], preferred_element_type=f32
        )
        gate, up = both[:, :units], both[:, units:]
        hidden = (gate / (1.0 + jnp.exp(-gate)) * up).astype(bf16)
        part_two[first : first + count, :] = jnp.dot(
            hidden, w_down_vmem[...], preferred_element_type=f32
        ).astype(bf16)

    back = WideScatter(mail, part_two, *buffers_two)
    feed(0, OWN_ROWS)
    wide.finish(0)
    feed(OWN_ROWS, 4 * HALF)
    back.start(0)
    wide.finish(1)
    feed(OWN_ROWS + 4 * HALF, 4 * HALF)
    back.start(1)
    back.relay()
    for half_index in (0, 1):
        first = half_index * HALF
        out_ref[first : first + HALF, :] = middle[first : first + HALF, :] + back.total(half_index)
    mail.drain()


def layer(
    tokens,
    attn_gain,
    query_gain,
    key_gain,
    mlp_gain,
    sink_keys,
    sink_values,
    pages_keys,
    pages_values,
    w_query,
    key_weight,
    value_weight,
    w_headgate,
    w_out,
    w_gate,
    w_up,
    w_down,
    cached,
    valid,
    sinks,
    reach,
    slots,
):
    bf16, f32 = jnp.bfloat16, jnp.float32
    requests, _, head = sink_keys.shape
    rows_total = requests * SPAN_TOKENS
    group = w_query.shape[1] // head
    query_rows = group * SPAN_TOKENS
    smem = pl.BlockSpec(memory_space=pltpu.SMEM)
    vmem = pl.BlockSpec(memory_space=pltpu.VMEM)
    hbm = pl.BlockSpec(memory_space=pl.ANY)
    own_pages, _, heads, _ = pages_keys.shape
    arrived = (heads * own_pages, PAGE, head)
    by_head = (heads, own_pages, PAGE, head)
    relays = (2, 2, own_pages // 2, PAGE, head)
    buffers = [pltpu.VMEM(shape, bf16) for shape in SCATTER_BUFFERS]
    wide_buffers = [pltpu.VMEM(shape, bf16) for shape in WIDE_BUFFERS]
    copies = (
        SCATTER_COPIES + GATHER_COPIES + 2 * EXCHANGE_COPIES + WIDE_GATHER_COPIES + WIDE_SCATTER_COPIES
    )
    cosine, sine = rope_offsets()
    return pl.pallas_call(
        layer_kernel,
        out_shape=(
            jax.ShapeDtypeStruct(tokens.shape, f32),
            jax.ShapeDtypeStruct((rows_total, head), bf16),
            jax.ShapeDtypeStruct((rows_total, head), bf16),
        ),
        in_specs=[smem] * 5 + [vmem] * 10 + [hbm] * 10,
        out_specs=(vmem, vmem, vmem),
        scratch_shapes=[
            pltpu.VMEM((w_query.shape[0], (group + 2) * head), bf16),
            pltpu.VMEM(w_headgate.shape, bf16),
            pltpu.VMEM(w_out.shape, bf16),
            pltpu.VMEM((w_gate.shape[0], 2 * w_gate.shape[1]), bf16),
            pltpu.VMEM(w_down.shape, bf16),
            pltpu.VMEM((rows_total, WIDTH), bf16),
            pltpu.VMEM((requests, query_rows, head), bf16),
            pltpu.VMEM((requests, NEAR, head), bf16),
            pltpu.VMEM((requests, NEAR, head), bf16),
            pltpu.VMEM((rows_total, w_headgate.shape[0]), f32),
            pltpu.VMEM(arrived, bf16),
            pltpu.VMEM(arrived, bf16),
            pltpu.VMEM((2, *pages_keys.shape), bf16),
            pltpu.VMEM(by_head, bf16),
            pltpu.VMEM(by_head, bf16),
            pltpu.VMEM(relays, bf16),
            pltpu.VMEM(relays, bf16),
            pltpu.VMEM((WINDOW_TOKENS, head), bf16),
            pltpu.VMEM((query_rows, NEAR + WINDOW_TOKENS), f32),
            pltpu.VMEM((query_rows, 128), f32),
            pltpu.VMEM((requests, query_rows, NEAR + WINDOW_TOKENS), bf16),
            pltpu.VMEM((requests, query_rows, 1), f32),
            pltpu.VMEM((requests, query_rows, head), f32),
            pltpu.VMEM((rows_total, group * head), bf16),
            pltpu.VMEM((rows_total, WIDTH), bf16),
            pltpu.VMEM((rows_total, WIDTH), bf16),
            pltpu.VMEM((rows_total, WIDTH), bf16),
            pltpu.VMEM(tokens.shape, f32),
            *buffers,
            *wide_buffers,
            pltpu.SemaphoreType.DMA((12,)),
            pltpu.SemaphoreType.DMA((copies,)),
            pltpu.SemaphoreType.DMA((copies,)),
        ],
        compiler_params=pltpu.CompilerParams(
            collective_id=1, has_side_effects=True, vmem_limit_bytes=63 * 1024 * 1024
        ),
        name="layer",
    )(
        cached,
        valid,
        sinks,
        reach,
        slots,
        tokens,
        attn_gain[None, :],
        query_gain[None, :],
        key_gain[None, :],
        mlp_gain[None, :],
        jnp.asarray(np.tile(rope_frequencies(), 2).astype(np.float32)[None, :]),
        jnp.asarray(cosine),
        jnp.asarray(sine),
        sink_keys,
        sink_values,
        pages_keys,
        pages_values,
        w_query,
        key_weight,
        value_weight,
        w_headgate,
        w_out,
        w_gate,
        w_up,
        w_down,
    )


def body(
    tokens,
    attn_gain,
    w_query,
    key_weight,
    value_weight,
    w_headgate,
    query_gain,
    key_gain,
    w_out,
    mlp_gain,
    w_gate,
    w_up,
    w_down,
    pooled_keys,
    pooled_values,
    sink_key_cache,
    sink_value_cache,
    cached_length,
    valid_length,
    sink_position_count,
    window,
    page_slot,
):
    output, fresh_keys, fresh_values = layer(
        tokens,
        attn_gain,
        query_gain,
        key_gain,
        mlp_gain,
        sink_key_cache[:, :, 0, :],
        sink_value_cache[:, :, 0, :],
        pooled_keys,
        pooled_values,
        w_query,
        key_weight,
        value_weight,
        w_headgate.T,
        w_out,
        w_gate,
        w_up,
        w_down,
        cached_length,
        valid_length,
        sink_position_count,
        window,
        page_slot[0],
    )
    offsets = jnp.arange(SPAN_TOKENS, dtype=jnp.int32)
    present = (offsets[None, :] < valid_length[:, None]).reshape(-1)[:, None, None]
    app_keys, app_values = (
        jnp.where(present, fresh[:, None, :], jnp.zeros((), fresh.dtype))
        for fresh in (fresh_keys, fresh_values)
    )
    return (output, app_keys, app_values)


def solution(mesh):
    in_specs = (
        P(("req", "tp"), None),
        P(),
        P(None, "tp"),
        P(None, "tp"),
        P(None, "tp"),
        P(None, "tp"),
        P(),
        P(),
        P("tp", None),
        P(),
        P(None, "tp"),
        P(None, "tp"),
        P("tp", None),
        P(("req", "tp"), None, None, None),
        P(("req", "tp"), None, None, None),
        P("req", None, "tp", None),
        P("req", None, "tp", None),
        P("req"),
        P("req"),
        P("req"),
        P("req"),
        P("req", None),
    )
    out_specs = (P(("req", "tp"), None), P("req", "tp", None), P("req", "tp", None))
    return jax.shard_map(body, mesh=mesh, in_specs=in_specs, out_specs=out_specs, check_vma=False)
```

```python
import functools
import math

import jax
import jax.numpy as jnp
import numpy as np
from jax import lax
from jax.experimental import pallas as pl
from jax.experimental.pallas import tpu as pltpu
from jax.sharding import PartitionSpec as P

WINDOW_TOKENS = 4096
SPAN_TOKENS = 256


EPSILON = 1e-06
ROPE_BASE = 1000000.0
NEG_FILL = -1e30

MESH = pl.DeviceIdType.MESH
ROWS = 64
WIDTH = 2048
PEERS = ((1, False), (3, False), (0, True), (1, True), (3, True))
CORES = 2
Z_GROUPS = 4


def ring_place(shift, flip):
    t = lax.axis_index("tp")
    x = lax.rem(t, 4)
    z = t // 4
    plane = 1 - z if flip else z
    return lax.rem(x + shift, 4) + 4 * plane


def beyond_place():
    req = lax.axis_index("req")
    t = lax.axis_index("tp")
    group = req // CORES
    z_group = lax.rem(group, Z_GROUPS)
    step = jnp.where(t // 4 == 1, 1, Z_GROUPS - 1)
    moved = group - z_group + lax.rem(z_group + step, Z_GROUPS)
    return {"req": moved * CORES + lax.rem(req, CORES), "tp": ring_place(0, True)}


def row_window(owner, first, count):
    return pl.ds(pl.multiple_of(owner * ROWS + first, 16), count)


class Mailer:
    def __init__(self, send_sems, recv_sems):
        self.send_sems, self.recv_sems = send_sems, recv_sems
        self.slots = {}
        self.sent = []

    def slot(self, name):
        return self.slots.setdefault(name, len(self.slots))

    def send(self, name, src, dst, target):
        k = self.slot(name)
        copy = pltpu.make_async_remote_copy(
            src_ref=src,
            dst_ref=dst,
            send_sem=self.send_sems.at[k],
            recv_sem=self.recv_sems.at[k],
            device_id=target if isinstance(target, dict) else {"tp": target},
            device_id_type=MESH,
        )
        copy.start()
        self.sent.append(copy)

    def wait(self, name, dst):
        k = self.slot(name)
        pltpu.make_async_remote_copy(
            src_ref=dst,
            dst_ref=dst,
            send_sem=self.send_sems.at[k],
            recv_sem=self.recv_sems.at[k],
            device_id={"tp": ring_place(0, True)},
            device_id_type=MESH,
        ).wait_recv()

    def drain(self):
        for copy in self.sent:
            copy.wait_send()
        self.sent = []


def meet_neighbours():
    barrier = pltpu.get_barrier_semaphore()
    for shift, flip in PEERS:
        pl.semaphore_signal(
            barrier, inc=1, device_id={"tp": ring_place(shift, flip)}, device_id_type=MESH
        )
    pl.semaphore_signal(barrier, inc=1, device_id=beyond_place(), device_id_type=MESH)
    pl.semaphore_wait(barrier, len(PEERS) + 1)


def add_into(part, owner, first, count, arrived):
    rows = row_window(owner, first, count)
    part[rows, :] = (
        part[rows, :].astype(jnp.float32) + arrived[...].astype(jnp.float32)
    ).astype(jnp.bfloat16)


class Scatter:
    def __init__(self, mail, tag, part, h1, h2, zb, b1, b2, za):
        self.mail, self.tag, self.part = mail, tag, part
        self.h1, self.h2, self.zb, self.b1, self.b2, self.za = h1, h2, zb, b1, b2, za
        self.right, self.left, self.across = ring_place(1, False), ring_place(3, False), ring_place(0, True)

    def rows(self, shift, flip, first, count):
        return self.part.at[row_window(ring_place(shift, flip), first, count), :]

    def put(self, name, src, dst, target):
        self.mail.send(self.tag + name, src, dst, target)

    def got(self, name, dst):
        self.mail.wait(self.tag + name, dst)

    def start_x(self, flip):
        f = int(flip)
        self.put(f"h1r{f}", self.rows(2, flip, 0, 16), self.h1.at[0, f], self.right)
        self.put(f"h1l{f}", self.rows(2, flip, 16, 16), self.h1.at[1, f], self.left)
        self.put(f"h2r{f}1", self.rows(1, flip, 16, 16), self.h2.at[0, f, 1], self.right)
        self.put(f"h2l{f}0", self.rows(3, flip, 0, 16), self.h2.at[1, f, 0], self.left)

    def start_z(self):
        for k, shift in enumerate((2, 1, 3)):
            self.put(f"zb{k}", self.rows(shift, True, 32, 32), self.zb.at[k], self.across)

    def relay_x(self, flip):
        f = int(flip)
        self.got(f"h1r{f}", self.h1.at[0, f])
        add_into(self.part, ring_place(1, flip), 0, 16, self.h1.at[0, f])
        self.put(f"h2r{f}0", self.rows(1, flip, 0, 16), self.h2.at[0, f, 0], self.right)
        self.got(f"h1l{f}", self.h1.at[1, f])
        add_into(self.part, ring_place(3, flip), 16, 16, self.h1.at[1, f])
        self.put(f"h2l{f}1", self.rows(3, flip, 16, 16), self.h2.at[1, f, 1], self.left)

    def relay_far(self):
        self.got("zb0", self.zb.at[0])
        add_into(self.part, ring_place(2, False), 32, 32, self.zb.at[0])
        self.put("b1r", self.rows(2, False, 32, 16), self.b1.at[0], self.right)
        self.put("b1l", self.rows(2, False, 48, 16), self.b1.at[1], self.left)
        self.got("zb1", self.zb.at[1])
        add_into(self.part, ring_place(1, False), 32, 32, self.zb.at[1])
        self.put("b2r1", self.rows(1, False, 48, 16), self.b2.at[0, 1], self.right)

    def relay_z(self):
        self.got("zb2", self.zb.at[2])
        add_into(self.part, ring_place(3, False), 32, 32, self.zb.at[2])
        self.put("b2l0", self.rows(3, False, 32, 16), self.b2.at[1, 0], self.left)

    def cross(self):
        for side, letter in ((0, "r"), (1, "l")):
            for half in (0, 1):
                self.got(f"h2{letter}1{half}", self.h2.at[side, 1, half])
        rows = row_window(self.across, 0, 32)
        self.part[rows, :] = (
            self.part[rows, :].astype(jnp.float32)
            + self.h2[0, 1].reshape(32, WIDTH).astype(jnp.float32)
            + self.h2[1, 1].reshape(32, WIDTH).astype(jnp.float32)
        ).astype(jnp.bfloat16)
        self.put("za", self.rows(0, True, 0, 32), self.za, self.across)
        self.put("zb3", self.rows(0, True, 32, 32), self.zb.at[3], self.across)

    def finish_relays(self):
        self.got("b1r", self.b1.at[0])
        add_into(self.part, ring_place(1, False), 32, 16, self.b1.at[0])
        self.put("b2r0", self.rows(1, False, 32, 16), self.b2.at[0, 0], self.right)
        self.got("b1l", self.b1.at[1])
        add_into(self.part, ring_place(3, False), 48, 16, self.b1.at[1])
        self.put("b2l1", self.rows(3, False, 48, 16), self.b2.at[1, 1], self.left)

    def upper(self):
        f32 = jnp.float32
        for side, letter in ((0, "r"), (1, "l")):
            for half in (0, 1):
                self.got(f"h2{letter}0{half}", self.h2.at[side, 0, half])
        upper = (
            self.part[row_window(ring_place(0, False), 0, 32), :].astype(f32)
            + self.h2[0, 0].reshape(32, WIDTH).astype(f32)
            + self.h2[1, 0].reshape(32, WIDTH).astype(f32)
        )
        self.got("za", self.za)
        return upper + self.za[...].astype(f32)

    def lower(self):
        f32 = jnp.float32
        for side, letter in ((0, "r"), (1, "l")):
            for half in (0, 1):
                self.got(f"b2{letter}{half}", self.b2.at[side, half])
        self.got("zb3", self.zb.at[3])
        return (
            self.part[row_window(ring_place(0, False), 32, 32), :].astype(f32)
            + self.b2[0].reshape(32, WIDTH).astype(f32)
            + self.b2[1].reshape(32, WIDTH).astype(f32)
            + self.zb[3].astype(f32)
        )


SCATTER_BUFFERS = [
    ((2, 2, 16, WIDTH)),
    ((2, 2, 2, 16, WIDTH)),
    ((4, 32, WIDTH)),
    ((2, 16, WIDTH)),
    ((2, 2, 16, WIDTH)),
    ((32, WIDTH)),
]
SCATTER_COPIES = 24


class Gather:
    def __init__(self, mail, tag, rows):
        self.mail, self.tag, self.rows = mail, tag, rows
        self.right, self.left, self.across = ring_place(1, False), ring_place(3, False), ring_place(0, True)

    def part(self, shift, flip, first, count):
        return self.rows.at[row_window(ring_place(shift, flip), first, count), :]

    def put(self, name, place, target):
        ref = self.part(*place)
        self.mail.send(self.tag + name, ref, ref, target)

    def got(self, name, place):
        self.mail.wait(self.tag + name, self.part(*place))

    def start(self):
        self.put("z0", (0, False, 0, 32), self.across)
        self.put("r0", (0, False, 32, 32), self.right)
        self.put("l0", (0, False, 32, 32), self.left)
        self.put("r1", (0, False, 0, 32), self.right)
        self.put("l1", (0, False, 0, 32), self.left)
        self.put("z1", (0, False, 32, 32), self.across)

    def relay_near(self):
        self.got("r0", (3, False, 32, 32))
        self.put("r2", (3, False, 32, 16), self.right)
        self.put("z2", (3, False, 32, 32), self.across)
        self.got("l0", (1, False, 32, 32))
        self.put("l2", (1, False, 48, 16), self.left)
        self.put("z3", (1, False, 32, 32), self.across)
        self.got("r1", (3, False, 0, 32))
        self.put("r4", (3, False, 0, 16), self.right)
        self.got("l1", (1, False, 0, 32))
        self.put("l4", (1, False, 16, 16), self.left)
        self.got("z0", (0, True, 0, 32))
        self.put("r3", (0, True, 0, 32), self.right)
        self.put("l3", (0, True, 0, 32), self.left)
        self.got("r2", (2, False, 32, 16))
        self.put("z4", (2, False, 32, 16), self.across)
        self.got("l2", (2, False, 48, 16))
        self.put("z5", (2, False, 48, 16), self.across)
        self.got("r4", (2, False, 0, 16))
        self.got("l4", (2, False, 16, 16))

    def relay_far(self):
        self.got("r3", (3, True, 0, 32))
        self.put("r5", (3, True, 0, 16), self.right)
        self.got("l3", (1, True, 0, 32))
        self.put("l5", (1, True, 16, 16), self.left)

    def finish(self):
        self.got("r5", (2, True, 0, 16))
        self.got("l5", (2, True, 16, 16))
        self.got("z1", (0, True, 32, 32))
        self.got("z2", (3, True, 32, 32))
        self.got("z3", (1, True, 32, 32))
        self.got("z4", (2, True, 32, 16))
        self.got("z5", (2, True, 48, 16))


GATHER_COPIES = 18
OWN_ROWS = 4 * ROWS
HALF = ROWS // 2


def x_place(shift):
    return lax.rem(lax.axis_index("tp") + shift, 4)


def wide_window(block, shift, half=None):
    x = x_place(shift)
    if block == 0:
        return pl.ds(pl.multiple_of(x * ROWS + (half or 0) * HALF, HALF), ROWS if half is None else HALF)
    return pl.ds(pl.multiple_of(OWN_ROWS + (block - 1) * 4 * HALF + x * HALF, HALF), HALF)


class WideGather:
    def __init__(self, mail, rows):
        self.mail, self.rows = mail, rows
        self.right, self.left = ring_place(1, False), ring_place(3, False)
        self.over = (ring_place(0, True), beyond_place())

    def put(self, name, shift, half, block, target):
        self.mail.send(
            "w" + name,
            self.rows.at[wide_window(0, shift, half), :],
            self.rows.at[wide_window(block, shift, half), :],
            target,
        )

    def got(self, name, shift, half, block):
        self.mail.wait("w" + name, self.rows.at[wide_window(block, shift, half), :])

    def start(self, half):
        self.put(f"r{half}", 0, half, 0, self.right)
        self.put(f"l{half}", 0, half, 0, self.left)
        self.put(f"z{half}0", 0, half, half + 1, self.over[half])

    def relay(self):
        for half in (0, 1):
            self.got(f"r{half}", 3, half, 0)
            if half == 0:
                self.put("rr", 3, half, 0, self.right)
            self.put(f"z{half}3", 3, half, half + 1, self.over[half])
            self.got(f"l{half}", 1, half, 0)
            if half == 1:
                self.put("ll", 1, half, 0, self.left)
            self.put(f"z{half}1", 1, half, half + 1, self.over[half])
        self.got("rr", 2, 0, 0)
        self.put("z02", 2, 0, 1, self.over[0])
        self.got("ll", 2, 1, 0)
        self.put("z12", 2, 1, 2, self.over[1])

    def finish(self, half):
        for shift in (0, 3, 1, 2):
            self.got(f"z{half}{shift}", shift, half, half + 1)


WIDE_GATHER_COPIES = 14


class WideScatter:
    def __init__(self, mail, part, arrived, hop_one, hop_two):
        self.mail, self.part, self.arrived = mail, part, arrived
        self.hop_one, self.hop_two = hop_one, hop_two
        self.right, self.left = ring_place(1, False), ring_place(3, False)
        self.over = (ring_place(0, True), beyond_place())

    def start(self, half):
        for k, shift in enumerate((2, 1, 3, 0)):
            self.mail.send(
                f"y{half}{k}",
                self.part.at[wide_window(half + 1, shift), :],
                self.arrived.at[half, k],
                self.over[half],
            )

    def fold(self, half, k, shift):
        self.mail.wait(f"y{half}{k}", self.arrived.at[half, k])
        self.add(shift, half, self.arrived[half, k])

    def add(self, shift, half, values):
        rows = wide_window(0, shift, half)
        self.part[rows, :] = (
            self.part[rows, :].astype(jnp.float32) + values.astype(jnp.float32)
        ).astype(jnp.bfloat16)

    def put(self, name, shift, half, dst, target):
        self.mail.send("y" + name, self.part.at[wide_window(0, shift, half), :], dst, target)

    def relay(self):
        self.fold(0, 0, 2)
        self.put("hr", 2, 0, self.hop_one.at[0], self.right)
        self.fold(1, 0, 2)
        self.put("hl", 2, 1, self.hop_one.at[1], self.left)
        self.fold(1, 1, 1)
        self.put("r1", 1, 1, self.hop_two.at[0, 1], self.right)
        self.fold(0, 1, 1)
        self.mail.wait("yhr", self.hop_one.at[0])
        self.add(1, 0, self.hop_one[0])
        self.put("r0", 1, 0, self.hop_two.at[0, 0], self.right)
        self.fold(0, 2, 3)
        self.put("l0", 3, 0, self.hop_two.at[1, 0], self.left)
        self.fold(1, 2, 3)
        self.mail.wait("yhl", self.hop_one.at[1])
        self.add(3, 1, self.hop_one[1])
        self.put("l1", 3, 1, self.hop_two.at[1, 1], self.left)

    def total(self, half):
        f32 = jnp.float32
        self.mail.wait(f"y{half}3", self.arrived.at[half, 3])
        self.mail.wait(f"yr{half}", self.hop_two.at[0, half])
        self.mail.wait(f"yl{half}", self.hop_two.at[1, half])
        return (
            self.part[wide_window(0, 0, half), :].astype(f32)
            + self.arrived[half, 3].astype(f32)
            + self.hop_two[0, half].astype(f32)
            + self.hop_two[1, half].astype(f32)
        )


WIDE_BUFFERS = [(2, 4, HALF, WIDTH), (2, HALF, WIDTH), (2, 2, HALF, WIDTH)]
WIDE_SCATTER_COPIES = 14


PAGE = 16
NEAR = 384
BLOCK = 512
ROPE_HALF = 64


def rope_frequencies():
    return ROPE_BASE ** (-np.arange(ROPE_HALF) / ROPE_HALF)


def rope_offsets():
    angles = np.arange(SPAN_TOKENS)[:, None] * rope_frequencies()[None, :]
    cosine, sine = np.cos(angles), np.sin(angles)
    return (
        np.concatenate([cosine, cosine], axis=1).astype(np.float32),
        np.concatenate([-sine, sine], axis=1).astype(np.float32),
    )


class Exchange:
    def __init__(self, mail, tag, pages, arrived, relays, own_sem):
        self.mail, self.tag, self.pages, self.arrived, self.relays = mail, tag, pages, arrived, relays
        self.count = pages.shape[1]
        me = ring_place(0, False)
        self.own = pltpu.make_async_copy(pages.at[me], self.slot(me, 0, self.count), own_sem)

    def slot(self, source, first, count):
        return self.arrived.at[pl.ds(source * self.count + first, count)]

    def start(self):
        half = self.count // 2
        me = ring_place(0, False)
        for flip in (False, True):
            target = self.pages.at[ring_place(2, flip)]
            f = int(flip)
            self.mail.send(
                f"{self.tag}hr{f}", target.at[:half], self.relays.at[0, f], ring_place(1, False)
            )
            self.mail.send(
                f"{self.tag}hl{f}", target.at[half:], self.relays.at[1, f], ring_place(3, False)
            )
        for name, shift, flip in (
            ("xr", 1, True),
            ("xl", 3, True),
            ("dz", 0, True),
            ("dr", 1, False),
            ("dl", 3, False),
        ):
            target = ring_place(shift, flip)
            self.mail.send(
                self.tag + name, self.pages.at[target], self.slot(me, 0, self.count), target
            )
        self.own.start()

    def relay(self):
        half = self.count // 2
        for flip in (False, True):
            f = int(flip)
            self.mail.wait(f"{self.tag}hr{f}", self.relays.at[0, f])
            self.mail.send(
                f"{self.tag}fr{f}",
                self.relays.at[0, f],
                self.slot(ring_place(3, False), 0, half),
                ring_place(1, flip),
            )
            self.mail.wait(f"{self.tag}hl{f}", self.relays.at[1, f])
            self.mail.send(
                f"{self.tag}fl{f}",
                self.relays.at[1, f],
                self.slot(ring_place(1, False), half, half),
                ring_place(3, flip),
            )

    def finish(self):
        half = self.count // 2
        self.own.wait()
        for name, shift, flip in (
            ("dr", 3, False),
            ("dl", 1, False),
            ("dz", 0, True),
            ("xr", 3, True),
            ("xl", 1, True),
        ):
            self.mail.wait(self.tag + name, self.slot(ring_place(shift, flip), 0, self.count))
        for flip in (False, True):
            f = int(flip)
            self.mail.wait(f"{self.tag}fr{f}", self.slot(ring_place(2, flip), 0, half))
            self.mail.wait(f"{self.tag}fl{f}", self.slot(ring_place(2, flip), half, half))


EXCHANGE_COPIES = 13


def layer_kernel(
    cached_ref,
    valid_ref,
    sinks_ref,
    reach_ref,
    slot_ref,
    tokens_ref,
    attn_gain_ref,
    query_gain_ref,
    key_gain_ref,
    mlp_gain_ref,
    freqs_ref,
    cosine_ref,
    sine_ref,
    sink_keys_ref,
    sink_values_ref,
    pages_keys_ref,
    pages_values_ref,
    w_query_ref,
    key_weight_ref,
    value_weight_ref,
    w_headgate_ref,
    w_out_ref,
    w_gate_ref,
    w_up_ref,
    w_down_ref,
    out_ref,
    fresh_keys_ref,
    fresh_values_ref,
    w_in_vmem,
    w_headgate_vmem,
    w_out_vmem,
    w_both_vmem,
    w_down_vmem,
    rows_in,
    queries,
    near_keys,
    near_values,
    gates,
    arrived_keys,
    arrived_values,
    raw_pages,
    head_keys,
    head_values,
    relay_keys,
    relay_values,
    window_rows,
    scores,
    peaks,
    weights,
    totals,
    near_sums,
    heads,
    part_one,
    part_two,
    rows_mid,
    middle,
    *rest,
):
    buffers_one, buffers_two = rest[:6], rest[6:9]
    load_sems, send_sems, recv_sems = rest[9:]
    f32, bf16 = jnp.float32, jnp.bfloat16
    units = w_down_ref.shape[0]
    head = key_weight_ref.shape[1]
    query_width = w_query_ref.shape[1]
    group = query_width // head
    span = SPAN_TOKENS
    query_rows = group * span
    pages = WINDOW_TOKENS // PAGE
    requests = cached_ref.shape[0]
    scale = 1.0 / math.sqrt(head)
    loads = [
        pltpu.make_async_copy(src, dst, load_sems.at[k])
        for k, (src, dst) in enumerate(
            (
                (w_query_ref, w_in_vmem.at[:, :query_width]),
                (key_weight_ref, w_in_vmem.at[:, query_width : query_width + head]),
                (value_weight_ref, w_in_vmem.at[:, query_width + head :]),
                (w_headgate_ref, w_headgate_vmem),
                (w_out_ref, w_out_vmem),
                (w_gate_ref, w_both_vmem.at[:, :units]),
                (w_up_ref, w_both_vmem.at[:, units:]),
                (w_down_ref, w_down_vmem),
            )
        )
    ]
    raw_loads = [
        pltpu.make_async_copy(pages_keys_ref, raw_pages.at[0], load_sems.at[10]),
        pltpu.make_async_copy(pages_values_ref, raw_pages.at[1], load_sems.at[11]),
    ]
    meet_neighbours()
    mail = Mailer(send_sems, recv_sems)
    plane = lax.axis_index("tp") // 4
    me = ring_place(0, False)

    def rms(values, gain):
        mean_square = jnp.mean(values * values, axis=-1, keepdims=True)
        return values * lax.rsqrt(mean_square + EPSILON) * gain

    rows_in[row_window(me, 0, ROWS), :] = rms(
        tokens_ref[...].astype(f32), attn_gain_ref[...]
    ).astype(bf16)
    gather = Gather(mail, "n", rows_in)
    gather.start()
    for load in raw_loads[:1] + loads[:4] + raw_loads[1:]:
        load.start()
    for member in range(requests):
        near_keys[member, span:, :] = jnp.zeros((NEAR - span, head), bf16)
        near_values[member, span:, :] = jnp.zeros((NEAR - span, head), bf16)
        sink_count = sink_keys_ref.shape[1]
        near_keys[member, span : span + sink_count, :] = sink_keys_ref[member]
        near_values[member, span : span + sink_count, :] = sink_values_ref[member]

    def by_head(which, target):
        raw_loads[which].wait()
        count = 8

        def step(index, carry):
            place = pl.ds(index * count, count)
            block = raw_pages[which, place].reshape(count * PAGE, *raw_pages.shape[3:])
            target[:, place] = jnp.swapaxes(block, 0, 1).reshape(-1, count, PAGE, head)
            return carry

        lax.fori_loop(0, raw_pages.shape[1] // count, step, 0)

    by_head(0, head_keys)
    gather.relay_near()
    gather.relay_far()
    exchange_keys = Exchange(mail, "k", head_keys, arrived_keys, relay_keys, load_sems.at[8])
    exchange_values = Exchange(
        mail, "v", head_values, arrived_values, relay_values, load_sems.at[9]
    )
    exchange_keys.start()
    for load in loads[:4]:
        load.wait()

    def enter(flip):
        member = 1 - plane if flip else plane
        rows = pl.ds(pl.multiple_of(member * span, span), span)
        normed = rows_in[rows, :]
        mixed = jnp.dot(normed, w_in_vmem[...], preferred_element_type=f32)
        logits = lax.dot_general(
            normed, w_headgate_vmem[...], (((1,), (1,)), ((), ())), preferred_element_type=f32
        )
        gates[rows, :] = 1.0 / (1.0 + jnp.exp(-logits))
        angles = cached_ref[member].astype(f32) * freqs_ref[...]
        lanes = lax.broadcasted_iota(jnp.int32, angles.shape, 1)
        base_cosine = jnp.cos(angles)
        base_sine = jnp.where(lanes < ROPE_HALF, -jnp.sin(angles), jnp.sin(angles))
        cosine = base_cosine * cosine_ref[...] - base_sine * sine_ref[...]
        sine = base_sine * cosine_ref[...] + base_cosine * sine_ref[...]

        def turn(values, gain):
            normed_head = rms(values, gain)
            return (
                normed_head * cosine + pltpu.roll(normed_head, ROPE_HALF, axis=1) * sine
            ).astype(bf16)

        for part in range(group):
            queries[member, part * span : (part + 1) * span, :] = turn(
                mixed[:, part * head : (part + 1) * head], query_gain_ref[...]
            )
        fresh_keys = turn(mixed[:, query_width : query_width + head], key_gain_ref[...])
        fresh_values = mixed[:, query_width + head :].astype(bf16)
        near_keys[member, :span, :] = fresh_keys
        near_values[member, :span, :] = fresh_values
        fresh_keys_ref[rows, :] = fresh_keys
        fresh_values_ref[rows, :] = fresh_values

    by_head(1, head_values)
    enter(False)
    gather.finish()
    exchange_keys.relay()
    exchange_values.start()
    for load in loads[4:]:
        load.start()
    enter(True)

    def fetch(member, arrived):
        count = 32

        def step(index, carry):
            slots = [slot_ref[member * pages + index * count + part] for part in range(count)]
            place = pl.ds(pl.multiple_of(index * count * PAGE, count * PAGE), count * PAGE)
            window_rows[place, :] = jnp.concatenate([arrived[slot] for slot in slots], axis=0)
            return carry

        lax.fori_loop(0, pages // count, step, 0)

    def lane_tiles(values):
        return [values[:, k : k + 128] for k in range(0, values.shape[1], 128)]

    def score(member):
        cached, valid = cached_ref[member], valid_ref[member]
        sinks, reach = sinks_ref[member], reach_ref[member]
        contract = (((1,), (1,)), ((), ()))
        row = lax.broadcasted_iota(jnp.int32, (query_rows, NEAR), 0)
        offset = jnp.where(row >= span, row - span, row)
        column = lax.broadcasted_iota(jnp.int32, (query_rows, NEAR), 1)
        sink = column - span
        span_ok = (
            (column < valid)
            & (column <= offset)
            & ((cached + column < sinks) | (offset - column <= reach))
        )
        sink_ok = (sink < sinks) & (sink < cached - WINDOW_TOKENS)
        allowed = ((column < span) & span_ok) | (
            (column >= span) & (sink < sink_keys_ref.shape[1]) & sink_ok
        )
        near = lax.dot_general(
            queries[member], near_keys[member], contract, preferred_element_type=f32
        )
        near = jnp.where(allowed, near * scale, NEG_FILL)
        scores[:, :NEAR] = near
        peaks[...] = functools.reduce(jnp.maximum, lane_tiles(near))

        def step(index, carry):
            keys = window_rows[pl.ds(pl.multiple_of(index * BLOCK, BLOCK), BLOCK), :]
            row = lax.broadcasted_iota(jnp.int32, (query_rows, BLOCK), 0)
            offset = jnp.where(row >= span, row - span, row)
            slot = lax.broadcasted_iota(jnp.int32, (query_rows, BLOCK), 1) + index * BLOCK
            position = slot + (cached - WINDOW_TOKENS)
            allowed = (position >= 0) & (
                (position < sinks) | (WINDOW_TOKENS - slot + offset <= reach)
            )
            block = lax.dot_general(queries[member], keys, contract, preferred_element_type=f32)
            block = jnp.where(allowed, block * scale, NEG_FILL)
            scores[:, pl.ds(pl.multiple_of(NEAR + index * BLOCK, 128), BLOCK)] = block
            peaks[...] = functools.reduce(jnp.maximum, lane_tiles(block), peaks[...])
            return carry

        lax.fori_loop(0, WINDOW_TOKENS // BLOCK, step, 0)
        peak = jnp.max(peaks[...], axis=-1, keepdims=True)

        def soften(place):
            block = jnp.exp(scores[:, place] - peak)
            weights[member, :, place] = block.astype(bf16)
            return functools.reduce(jnp.add, lane_tiles(block))

        peaks[...] = soften(pl.ds(0, NEAR))

        def soft_step(index, carry):
            peaks[...] += soften(pl.ds(pl.multiple_of(NEAR + index * BLOCK, 128), BLOCK))
            return carry

        lax.fori_loop(0, WINDOW_TOKENS // BLOCK, soft_step, 0)
        totals[member] = jnp.sum(peaks[...], axis=-1, keepdims=True)
        near_sums[member] = jnp.dot(
            weights[member, :, :NEAR], near_values[member], preferred_element_type=f32
        )

    exchange_keys.finish()
    fetch(0, arrived_keys)
    score(0)
    exchange_values.relay()
    fetch(1, arrived_keys)
    score(1)
    exchange_values.finish()

    def mix(flip):
        member = 1 - plane if flip else plane
        fetch(member, arrived_values)
        summed = near_sums[member] + jnp.dot(
            weights[member, :, NEAR:], window_rows[...], preferred_element_type=f32
        )
        mixture = summed / totals[member]
        rows = pl.ds(pl.multiple_of(member * span, span), span)
        for part in range(group):
            heads[rows, part * head : (part + 1) * head] = (
                mixture[part * span : (part + 1) * span, :] * gates[rows, part : part + 1]
            ).astype(bf16)

    half_rows = 4 * ROWS

    def half(flip):
        return pl.ds(pl.multiple_of((1 - plane if flip else plane) * half_rows, half_rows), half_rows)

    scatter = Scatter(mail, "a", part_one, *buffers_one)
    loads[4].wait()

    def project(flip):
        rows = half(flip)
        part_one[rows, :] = jnp.dot(
            heads[rows, :], w_out_vmem[...], preferred_element_type=f32
        ).astype(bf16)

    mix(True)
    project(True)
    scatter.start_z()
    scatter.start_x(True)
    mix(False)
    project(False)
    scatter.start_x(False)
    scatter.relay_x(True)
    scatter.relay_x(False)
    scatter.relay_far()
    scatter.cross()
    scatter.relay_z()
    scatter.finish_relays()
    wide = WideGather(mail, rows_mid)

    def settle(half_index, attn):
        first = half_index * HALF
        mid = tokens_ref[first : first + HALF, :].astype(f32) + attn
        middle[first : first + HALF, :] = mid
        rows_mid[wide_window(0, 0, half_index), :] = rms(mid, mlp_gain_ref[...]).astype(bf16)
        wide.start(half_index)

    settle(0, scatter.upper())
    settle(1, scatter.lower())
    wide.relay()
    for load in loads[5:]:
        load.wait()

    def feed(first, count):
        both = jnp.dot(
            rows_mid[first : first + count, :], w_both_vmem[...], preferred_element_type=f32
        )
        gate, up = both[:, :units], both[:, units:]
        hidden = (gate / (1.0 + jnp.exp(-gate)) * up).astype(bf16)
        part_two[first : first + count, :] = jnp.dot(
            hidden, w_down_vmem[...], preferred_element_type=f32
        ).astype(bf16)

    back = WideScatter(mail, part_two, *buffers_two)
    feed(0, OWN_ROWS)
    wide.finish(0)
    feed(OWN_ROWS, 4 * HALF)
    back.start(0)
    wide.finish(1)
    feed(OWN_ROWS + 4 * HALF, 4 * HALF)
    back.start(1)
    back.relay()
    for half_index in (0, 1):
        first = half_index * HALF
        out_ref[first : first + HALF, :] = middle[first : first + HALF, :] + back.total(half_index)
    mail.drain()


def layer(
    tokens,
    attn_gain,
    query_gain,
    key_gain,
    mlp_gain,
    sink_keys,
    sink_values,
    pages_keys,
    pages_values,
    w_query,
    key_weight,
    value_weight,
    w_headgate,
    w_out,
    w_gate,
    w_up,
    w_down,
    cached,
    valid,
    sinks,
    reach,
    slots,
):
    bf16, f32 = jnp.bfloat16, jnp.float32
    requests, _, head = sink_keys.shape
    rows_total = requests * SPAN_TOKENS
    group = w_query.shape[1] // head
    query_rows = group * SPAN_TOKENS
    smem = pl.BlockSpec(memory_space=pltpu.SMEM)
    vmem = pl.BlockSpec(memory_space=pltpu.VMEM)
    hbm = pl.BlockSpec(memory_space=pl.ANY)
    own_pages, _, heads, _ = pages_keys.shape
    arrived = (heads * own_pages, PAGE, head)
    by_head = (heads, own_pages, PAGE, head)
    relays = (2, 2, own_pages // 2, PAGE, head)
    buffers = [pltpu.VMEM(shape, bf16) for shape in SCATTER_BUFFERS]
    wide_buffers = [pltpu.VMEM(shape, bf16) for shape in WIDE_BUFFERS]
    copies = (
        SCATTER_COPIES + GATHER_COPIES + 2 * EXCHANGE_COPIES + WIDE_GATHER_COPIES + WIDE_SCATTER_COPIES
    )
    cosine, sine = rope_offsets()
    return pl.pallas_call(
        layer_kernel,
        out_shape=(
            jax.ShapeDtypeStruct(tokens.shape, f32),
            jax.ShapeDtypeStruct((rows_total, head), bf16),
            jax.ShapeDtypeStruct((rows_total, head), bf16),
        ),
        in_specs=[smem] * 5 + [vmem] * 10 + [hbm] * 10,
        out_specs=(vmem, vmem, vmem),
        scratch_shapes=[
            pltpu.VMEM((w_query.shape[0], (group + 2) * head), bf16),
            pltpu.VMEM(w_headgate.shape, bf16),
            pltpu.VMEM(w_out.shape, bf16),
            pltpu.VMEM((w_gate.shape[0], 2 * w_gate.shape[1]), bf16),
            pltpu.VMEM(w_down.shape, bf16),
            pltpu.VMEM((rows_total, WIDTH), bf16),
            pltpu.VMEM((requests, query_rows, head), bf16),
            pltpu.VMEM((requests, NEAR, head), bf16),
            pltpu.VMEM((requests, NEAR, head), bf16),
            pltpu.VMEM((rows_total, w_headgate.shape[0]), f32),
            pltpu.VMEM(arrived, bf16),
            pltpu.VMEM(arrived, bf16),
            pltpu.VMEM((2, *pages_keys.shape), bf16),
            pltpu.VMEM(by_head, bf16),
            pltpu.VMEM(by_head, bf16),
            pltpu.VMEM(relays, bf16),
            pltpu.VMEM(relays, bf16),
            pltpu.VMEM((WINDOW_TOKENS, head), bf16),
            pltpu.VMEM((query_rows, NEAR + WINDOW_TOKENS), f32),
            pltpu.VMEM((query_rows, 128), f32),
            pltpu.VMEM((requests, query_rows, NEAR + WINDOW_TOKENS), bf16),
            pltpu.VMEM((requests, query_rows, 1), f32),
            pltpu.VMEM((requests, query_rows, head), f32),
            pltpu.VMEM((rows_total, group * head), bf16),
            pltpu.VMEM((rows_total, WIDTH), bf16),
            pltpu.VMEM((rows_total, WIDTH), bf16),
            pltpu.VMEM((rows_total, WIDTH), bf16),
            pltpu.VMEM(tokens.shape, f32),
            *buffers,
            *wide_buffers,
            pltpu.SemaphoreType.DMA((12,)),
            pltpu.SemaphoreType.DMA((copies,)),
            pltpu.SemaphoreType.DMA((copies,)),
        ],
        compiler_params=pltpu.CompilerParams(
            collective_id=1, has_side_effects=True, vmem_limit_bytes=63 * 1024 * 1024
        ),
        name="layer",
    )(
        cached,
        valid,
        sinks,
        reach,
        slots,
        tokens,
        attn_gain[None, :],
        query_gain[None, :],
        key_gain[None, :],
        mlp_gain[None, :],
        jnp.asarray(np.tile(rope_frequencies(), 2).astype(np.float32)[None, :]),
        jnp.asarray(cosine),
        jnp.asarray(sine),
        sink_keys,
        sink_values,
        pages_keys,
        pages_values,
        w_query,
        key_weight,
        value_weight,
        w_headgate,
        w_out,
        w_gate,
        w_up,
        w_down,
    )


def body(
    tokens,
    attn_gain,
    w_query,
    key_weight,
    value_weight,
    w_headgate,
    query_gain,
    key_gain,
    w_out,
    mlp_gain,
    w_gate,
    w_up,
    w_down,
    pooled_keys,
    pooled_values,
    sink_key_cache,
    sink_value_cache,
    cached_length,
    valid_length,
    sink_position_count,
    window,
    page_slot,
):
    output, fresh_keys, fresh_values = layer(
        tokens,
        attn_gain,
        query_gain,
        key_gain,
        mlp_gain,
        sink_key_cache[:, :, 0, :],
        sink_value_cache[:, :, 0, :],
        pooled_keys,
        pooled_values,
        w_query,
        key_weight,
        value_weight,
        w_headgate.T,
        w_out,
        w_gate,
        w_up,
        w_down,
        cached_length,
        valid_length,
        sink_position_count,
        window,
        page_slot[0],
    )
    offsets = jnp.arange(SPAN_TOKENS, dtype=jnp.int32)
    present = (offsets[None, :] < valid_length[:, None]).reshape(-1)[:, None, None]
    app_keys, app_values = (
        jnp.where(present, fresh[:, None, :], jnp.zeros((), fresh.dtype))
        for fresh in (fresh_keys, fresh_values)
    )
    return (output, app_keys, app_values)


def solution(mesh):
    in_specs = (
        P(("req", "tp"), None),
        P(),
        P(None, "tp"),
        P(None, "tp"),
        P(None, "tp"),
        P(None, "tp"),
        P(),
        P(),
        P("tp", None),
        P(),
        P(None, "tp"),
        P(None, "tp"),
        P("tp", None),
        P(("req", "tp"), None, None, None),
        P(("req", "tp"), None, None, None),
        P("req", None, "tp", None),
        P("req", None, "tp", None),
        P("req"),
        P("req"),
        P("req"),
        P("req"),
        P("req", None),
    )
    out_specs = (P(("req", "tp"), None), P("req", "tp", None), P("req", "tp", None))
    return jax.shard_map(body, mesh=mesh, in_specs=in_specs, out_specs=out_specs, check_vma=False)
```
